512 devices in a mesh: row: 8 (over x, y_lo), col: 16 (over z), rep: 4 (over y_hi, core).
Axes of the slice: x: 4, y: 4 (y_hi: 2, y_lo: 2; y = y_hi * 2 + y_lo), z: 16, core: 2. Of those that a mesh axis runs over, the one named last changes fastest.
Arguments:
- features: float32 [262144, 256], P(('row', 'col', 'rep')), may hold values from -6 to 6
- self_weight: float32 [256, 256], replicated, may hold values from -0.375 to 0.375
- neigh_weight: float32 [256, 256], replicated, may hold values from -1.2 to 1.2
- block_source: int32 [4096, 8], P(('row', 'col', 'rep')), may hold values from 0 to 95, as said below
- edge_weights: int32 [4096, 8, 64, 64], P(('row', 'col', 'rep')), may hold values from 0 to 15, as said below
- labels: int32 [262144], P(('row', 'col', 'rep')), may hold values from 0 to 255
Outputs:
- grad_self: float32 [256, 256], replicated
- grad_neigh: float32 [256, 256], replicated
- grad_features: float32 [262144, 256], P(('row', 'col', 'rep'))
The draws below stay inside these ranges and needn't reach their ends.
Inputs may be any that keep to these rules, and one draw needn't show every extreme that they name: `block_source`: slot 0 of every block row names the row's own block. `edge_weights`: in each block row the filled slots come first, with entries 1 to 15; later slots are all zero. Every block row has 1 to 8 filled slots, and some block row has all 8.
All inputs are finite; a program needn't handle non-finite values.
Results may differ from the reference program's by a relative error of at most 0.0035.
Values may be sent and summed in bfloat16 or wider, within the bound.
A program may use at most 64 MiB of HBM per device.

```python
import jax
import jax.numpy as jnp
from jax import lax

FEAT = 256
CLASSES = 256
BLOCK = 64
SLOTS = 8
ROWS_DEV = 512
GROUP = 2048
NODES = 262144
BLOCKS = 4096
N_COL = 16
N_REP = 4


def slot_counts(key):
    block_count = ROWS_DEV // BLOCK
    device_total = NODES // ROWS_DEV
    first_key, second_key, third_key, fourth_key = jax.random.split(jax.random.fold_in(key, 11), 4)
    level = jax.random.randint(first_key, (device_total,), 2, SLOTS + 1)
    chosen = jax.random.randint(second_key, (), 0, device_total)
    level = jnp.where(jnp.arange(device_total) == chosen, SLOTS, level)
    per_block = jnp.repeat(level, block_count)
    lowest = jnp.maximum(per_block - 3, 1)
    counts = jax.random.randint(third_key, (BLOCKS,), lowest, per_block + 1)
    target_spot = chosen * block_count + jax.random.randint(fourth_key, (), 0, block_count)
    return jnp.where(jnp.arange(BLOCKS) == target_spot, SLOTS, counts)


def draw_edge_weights(key, part):
    counts = slot_counts(key)
    values = jax.random.randint(jax.random.fold_in(key, 23), (BLOCKS, SLOTS, BLOCK, BLOCK), 1, 16)
    filled = jnp.arange(SLOTS)[None, :] < counts[:, None]
    return jnp.where(filled[:, :, None, None], values, 0).astype(jnp.int32)


def draw_block_source(key, part):
    group_blocks = GROUP // BLOCK
    sources = jax.random.randint(jax.random.fold_in(key, 37), (BLOCKS, SLOTS), 0, 3 * group_blocks)
    own_block = jnp.arange(BLOCKS) % group_blocks
    return sources.at[:, 0].set(own_block).astype(jnp.int32)


def touch_ends(values, key, low, top_value):
    extent = values.shape
    index_at = [jax.random.randint(jax.random.fold_in(key, axis), (), 0, extent[axis]) for axis in range(len(extent))]
    values = values.at[tuple(index_at)].set(low)
    longest = extent.index(max(extent))
    index_at[longest] = (index_at[longest] + 1) % extent[longest]
    return values.at[tuple(index_at)].set(top_value)


def shard_levels(rng, dims, cuts, low, top_value):
    factor_of = 1.0
    for dim, shards_of in cuts:
        steps = jax.random.uniform(jax.random.fold_in(jax.random.fold_in(rng, 6), dim), (shards_of,), jnp.float32, low / len(cuts), top_value / len(cuts))
        factor_of = factor_of * jnp.repeat(jnp.exp(steps), dims[dim] // shards_of).reshape((-1,) + (1,) * (len(dims) - 1 - dim))
    return factor_of


def bell_draw(own_key, shape, scale, reach, pieces=(), kind=jnp.bfloat16):
    gain = shard_levels(own_key, shape, pieces, -0.22, 0.18) if pieces else 1.0
    entries = jax.random.normal(own_key, shape, jnp.float32) * scale * gain
    return jnp.minimum(jnp.maximum(entries, -reach), reach).astype(kind)


def setup_inputs(seed: int = 0) -> dict:
    splits = jax.random.split(jax.random.key(seed), 7)
    return {
        "features": bell_draw(splits[0], (NODES, FEAT), 1.0, 6.0, ((0, 512),), jnp.float32),
        "self_weight": bell_draw(splits[1], (FEAT, CLASSES), FEAT ** -0.5, 0.375, (), jnp.float32),
        "neigh_weight": bell_draw(splits[2], (FEAT, CLASSES), 0.2, 1.2, (), jnp.float32),
        "block_source": draw_block_source(jax.random.fold_in(splits[6], 71), 0),
        "edge_weights": draw_edge_weights(jax.random.fold_in(splits[6], 71), 0),
        "labels": touch_ends(jax.random.randint(splits[5], (NODES,), 0, CLASSES), jax.random.fold_in(splits[5], 1), 0, CLASSES - 1).astype(jnp.int32),
    }


def reference(features, self_weight, neigh_weight, block_source, edge_weights, labels):
    high = lax.Precision.HIGHEST
    block_total = NODES // BLOCK
    block_count = ROWS_DEV // BLOCK
    group_blocks = GROUP // BLOCK
    device_total = NODES // ROWS_DEV
    lowered = lax.optimization_barrier(features.astype(jnp.bfloat16)).astype(jnp.float32)
    table = lowered.reshape(block_total, BLOCK, FEAT)
    device_ids = jnp.arange(device_total, dtype=jnp.int32)
    region = device_ids // N_REP
    region_row = region // N_COL
    region_col = region % N_COL
    peer_regions = jnp.stack([region, region_row * N_COL + (region_col - 1) % N_COL, region_row * N_COL + (region_col + 1) % N_COL], axis=1).astype(jnp.int32)
    source_dev = block_source.reshape(device_total, block_count, SLOTS).astype(jnp.int32)
    global_source = (peer_regions[device_ids[:, None, None], source_dev // group_blocks] * group_blocks + source_dev % group_blocks).astype(jnp.int32)
    weights_dev = edge_weights.reshape(device_total, block_count, SLOTS, BLOCK, BLOCK)
    degree = jnp.sum(edge_weights, axis=(1, 3)).astype(jnp.float32)

    def aggregate_device(inputs):
        weight_tiles, sources = inputs
        return jnp.einsum("bsij,bsjf->bif", weight_tiles.astype(jnp.float32), table[sources], precision=high)

    aggregated = lax.map(aggregate_device, (weights_dev, global_source))
    neighbour_mean = (aggregated.reshape(block_total, BLOCK, FEAT) / degree[..., None]).reshape(NODES, FEAT)
    logits = jnp.dot(features, self_weight, precision=high) + jnp.dot(neighbour_mean, neigh_weight, precision=high)
    target = (labels[:, None] == jnp.arange(CLASSES, dtype=jnp.int32)[None, :]).astype(jnp.float32)
    residual = jax.nn.sigmoid(logits) - target
    grad_self = jnp.dot(features.T, residual, precision=high)
    grad_neigh = jnp.dot(neighbour_mean.T, residual, precision=high)
    spread = jnp.dot(residual, neigh_weight.T, precision=high).reshape(block_total, BLOCK, FEAT) / degree[..., None]
    spread = lax.optimization_barrier(spread.astype(jnp.bfloat16)).astype(jnp.float32)
    spread_dev = spread.reshape(device_total, block_count, BLOCK, FEAT)

    def back_device(running, inputs):
        weight_tiles, sources, spread_rows, peers = inputs
        contrib = jnp.einsum("bsij,bif->bsjf", weight_tiles.astype(jnp.float32), spread_rows, precision=high)
        partial_sum = jnp.zeros((3 * group_blocks, BLOCK, FEAT), jnp.float32)
        partial_sum = partial_sum.at[sources.reshape(-1)].add(contrib.reshape(-1, BLOCK, FEAT))
        partial_sum = lax.optimization_barrier(partial_sum.astype(jnp.bfloat16)).astype(jnp.float32)
        target_blocks = (peers[:, None] * group_blocks + jnp.arange(group_blocks, dtype=jnp.int32)[None, :]).reshape(-1).astype(jnp.int32)
        return running.at[target_blocks].add(partial_sum), None

    returned, unused = lax.scan(back_device, jnp.zeros((block_total, BLOCK, FEAT), jnp.float32), (weights_dev, source_dev, spread_dev, peer_regions))
    grad_features = jnp.dot(residual, self_weight.T, precision=high) + returned.reshape(NODES, FEAT)
    return (grad_self, grad_neigh, grad_features)
```

```python
import functools

import jax
import jax.numpy as jnp
from jax import lax
from jax.experimental import pallas as pl
from jax.experimental.pallas import tpu as pltpu
from jax.sharding import PartitionSpec as P

MESH = pl.DeviceIdType.MESH
BF = jnp.bfloat16
F32 = jnp.float32
BLOCK = 64
ROWS = 512
NK = 4
CH = ROWS // NK
ORDER = (0, 2, 1, 3)
HIGH = lax.Precision.HIGHEST
DMA = pltpu.SemaphoreType.DMA
VM = pl.BlockSpec(memory_space=pltpu.VMEM)
SM = pl.BlockSpec(memory_space=pltpu.SMEM)


def remote(src, dst, ssem, rsem, dev):
    return pltpu.make_async_remote_copy(
        src_ref=src, dst_ref=dst, send_sem=ssem, recv_sem=rsem, device_id=dev, device_id_type=MESH
    )


class Place:
    def __init__(self, nx, nz):
        self.nx, self.nz = nx, nz
        row, self.z, self.rep = lax.axis_index("row"), lax.axis_index("col"), lax.axis_index("rep")
        self.x, self.ylo = row // 2, row % 2
        self.yhi, self.core = self.rep // 2, self.rep % 2
        self.y = self.yhi * 2 + self.ylo
        self.row = row

    def at(self, x, y, z, core):
        return {"row": x * 2 + y % 2, "col": z, "rep": (y // 2) * 2 + core}

    def partner(self):
        return self.at(self.x, self.y, self.z, 1 - self.core)

    def ystep(self, d):
        return self.at(self.x, (self.y + d) % 4, self.z, self.core)

    def zto(self, z):
        return self.at(self.x, self.y, z, self.core)

    def zstep(self, d):
        return self.zto((self.z + d) % self.nz)


def signal(devs):
    barrier = pltpu.get_barrier_semaphore()
    for dev in devs:
        pl.semaphore_signal(barrier, inc=1, device_id=dev, device_id_type=MESH)
    return barrier


def rows(k):
    return pl.ds(k * CH, CH)


def gather_kernel(nx, nz, f_ref, t_ref, relay, ps, pr, zs, zr, ys, yr, rs, rr):
    me = Place(nx, nz)
    partner = me.partner()
    up, down = me.zstep(1), me.zstep(nz - 1)
    yup, ydown = me.ystep(1), me.ystep(3)
    barrier = signal((partner, up, down, yup, ydown))
    rep = me.rep
    other = (1 - me.yhi) * 2 + me.core
    t_ref[rep] = f_ref[...].astype(BF)
    pl.semaphore_wait(barrier, 5)

    started = []

    def go(copy):
        copy.start()
        started.append(copy)

    def slot(m, mine, across):
        return (mine, across, 4 + mine, 8 + mine, 4 + across, 8 + across)[m]

    def to_partner(m, k):
        ref = t_ref.at[slot(m, rep, other), rows(k)]
        go(remote(ref, ref, ps.at[m, k], pr.at[m, k], partner))

    def from_partner(m, k):
        prep, pother = me.yhi * 2 + 1 - me.core, (1 - me.yhi) * 2 + 1 - me.core
        ref = t_ref.at[slot(m, prep, pother), rows(k)]
        remote(ref, ref, ps.at[m, k], pr.at[m, k], partner).wait_recv()

    def to_z(half, k):
        mine = (rep, other)[half]
        src = t_ref.at[mine, rows(k)]
        go(remote(src, t_ref.at[4 + mine, rows(k)], zs.at[0, half, k], zr.at[0, half, k], up))
        go(remote(src, t_ref.at[8 + mine, rows(k)], zs.at[1, half, k], zr.at[1, half, k], down))

    def z_arrived(half, k):
        mine = (rep, other)[half]
        for d in (0, 1):
            ref = t_ref.at[4 + 4 * d + mine, rows(k)]
            remote(ref, ref, zs.at[d, half, k], zr.at[d, half, k], up).wait_recv()
            to_partner(2 + 2 * half + d, k)

    def ydev(k):
        return yup if k < 2 else ydown

    def to_relay(k):
        go(remote(t_ref.at[rep, rows(k)], relay.at[rows(k)], ys.at[k], rr.at[k], ydev(k)))

    def relay_on(k):
        ref = relay.at[rows(k)]
        remote(ref, ref, ys.at[k], rr.at[k], yup).wait_recv()
        origin = (me.y + (3 if k < 2 else 1)) % 4
        dst = t_ref.at[(origin // 2) * 2 + me.core, rows(k)]
        go(remote(ref, dst, rs.at[k], yr.at[k], ydev(k)))

    def y_arrived(k):
        ref = t_ref.at[other, rows(k)]
        remote(ref, ref, rs.at[k], yr.at[k], yup).wait_recv()
        to_z(1, k)
        to_partner(1, k)

    for k in ORDER:
        to_relay(k)
        to_z(0, k)
    for k in ORDER:
        to_partner(0, k)
    relay_on(0)
    relay_on(2)
    z_arrived(0, 0)
    relay_on(1)
    relay_on(3)
    z_arrived(0, 2)
    y_arrived(0)
    y_arrived(2)
    z_arrived(0, 1)
    y_arrived(1)
    y_arrived(3)
    z_arrived(0, 3)
    for k in ORDER:
        z_arrived(1, k)
    for m in range(6):
        for k in ORDER:
            from_partner(m, k)
    for copy in started:
        copy.wait_send()


def gather(nx, nz, features):
    return pl.pallas_call(
        functools.partial(gather_kernel, nx, nz),
        out_shape=jax.ShapeDtypeStruct((12, ROWS, 256), BF),
        in_specs=[VM],
        out_specs=VM,
        scratch_shapes=[
            pltpu.VMEM((ROWS, 256), BF),
            DMA((6, NK)),
            DMA((6, NK)),
            DMA((2, 2, NK)),
            DMA((2, 2, NK)),
            DMA((NK,)),
            DMA((NK,)),
            DMA((NK,)),
            DMA((NK,)),
        ],
        compiler_params=pltpu.CompilerParams(collective_id=0, has_side_effects=True),
        name="gather_tables",
    )(features)


def dot(a, b, dims=((1,), (0,)), precision=None):
    return lax.dot_general(
        a, b, (dims, ((), ())), precision=precision, preferred_element_type=F32
    )


def local_kernel(
    src, fill, t_ref, f_ref, ws_ref, wn_ref, ew_ref, lab_ref, terms_ref, grads_ref, own_ref, acc, mean, deg, touched
):
    wide = []
    ones = jnp.ones((8 * BLOCK, 256), BF)
    for b in range(8):
        cat = jnp.concatenate([ew_ref[b, s].astype(F32).astype(BF) for s in range(8)], axis=1)
        wide.append(cat)
        table = jnp.concatenate([t_ref[src[b, s]] for s in range(8)], axis=0)
        d = dot(cat, ones)
        here = pl.ds(b * BLOCK, BLOCK)
        deg[here, :] = d
        mean[here, :] = dot(cat, table) / d
    feats, m = f_ref[...], mean[...]
    logits = dot(feats, ws_ref[...], precision=HIGH) + dot(m, wn_ref[...], precision=HIGH)
    label = jnp.broadcast_to(lab_ref[...].astype(F32), (256, ROWS)).T
    column = lax.broadcasted_iota(jnp.int32, (ROWS, 256), 1).astype(F32)
    residual = 1.0 / (1.0 + jnp.exp(-logits)) - jnp.where(label == column, 1.0, 0.0)
    turn = ((0,), (0,))
    last = ((1,), (1,))
    for i, left in enumerate((feats, m)):
        part = dot(left, residual, turn, precision=HIGH)
        for h in (0, 1):
            grads_ref[h, i * 256 : (i + 1) * 256, :] = part[:, h * 128 : (h + 1) * 128]
    own_ref[...] = dot(residual, ws_ref[...], last, precision=HIGH)
    spread = (dot(residual, wn_ref[...], last, precision=HIGH) / deg[...]).astype(BF)

    @pl.loop(0, 96)
    def _(t):
        touched[t] = 0

    for b in range(8):
        flipped = wide[b].astype(F32).T.astype(BF)
        contrib = dot(flipped, spread[b * BLOCK : (b + 1) * BLOCK, :])
        for s in range(8):
            mine = contrib[s * BLOCK : (s + 1) * BLOCK, :]
            t = src[b, s]

            @pl.when(fill[b, s] > 0)
            def _():
                @pl.when(touched[t] == 0)
                def _():
                    acc[t] = mine

                @pl.when(touched[t] > 0)
                def _():
                    acc[t] += mine

                touched[t] = 1

    @pl.loop(0, 96)
    def _(t):
        @pl.when(touched[t] > 0)
        def _():
            terms_ref[t] = acc[t].astype(BF)

        @pl.when(touched[t] == 0)
        def _():
            terms_ref[t] = jnp.zeros((BLOCK, 256), BF)


def local(table, features, self_weight, neigh_weight, block_source, edge_weights, labels):
    fill = (edge_weights[:, :, 0, 0] > 0).astype(jnp.int32)
    return pl.pallas_call(
        local_kernel,
        out_shape=(
            jax.ShapeDtypeStruct((96, BLOCK, 256), BF),
            jax.ShapeDtypeStruct((2, ROWS, 128), F32),
            jax.ShapeDtypeStruct((ROWS, 256), F32),
        ),
        in_specs=[SM, SM] + [VM] * 6,
        out_specs=(VM, VM, VM),
        scratch_shapes=[
            pltpu.VMEM((96, BLOCK, 256), F32),
            pltpu.VMEM((ROWS, 256), F32),
            pltpu.VMEM((ROWS, 256), F32),
            pltpu.SMEM((96,), jnp.int32),
        ],
        compiler_params=pltpu.CompilerParams(vmem_limit_bytes=48 << 20),
        name="local_math",
    )(
        block_source,
        fill,
        table.reshape(96, BLOCK, 256),
        features,
        self_weight,
        neigh_weight,
        edge_weights,
        labels.reshape(1, ROWS),
    )


def reduce_kernel(
    nx, nz, tm_ref, g_ref, own_ref, gs_ref, gn_ref, out_ref,
    pair, zsend, zgot, ysend, relay, ygot, gpair, total, plane, quad, far, part, full,
    ps, pr, zs, zr, ys, yr, rs, rr, gps, gpr, pls, plr, qs, qr, fs, fr, aqs, aqr, aps, apr, gfs, gfr,
):
    me = Place(nx, nz)
    partner = me.partner()
    core, yhi, z = me.core, me.yhi, me.z
    up, down = me.zstep(1), me.zstep(nz - 1)
    yup, ydown = me.ystep(1), me.ystep(3)
    flat = me.x * 4 + me.y
    q, h = z % 4, z // 4
    far_n = nz // 4
    planes = nx * 4

    def plane_dev(p):
        return me.at(p // 4, p % 4, z, core)

    barrier = signal((partner, up, down))

    @pl.loop(1, planes)
    def _(d):
        pl.semaphore_signal(barrier, inc=1, device_id=plane_dev((flat + d) % planes), device_id_type=MESH)

    for d in range(1, 4):
        pl.semaphore_signal(barrier, inc=1, device_id=me.zto(h * 4 + (q + d) % 4), device_id_type=MESH)
    for d in range(1, far_n):
        pl.semaphore_signal(barrier, inc=1, device_id=me.zto((h + d) % far_n * 4 + q), device_id_type=MESH)
    pl.semaphore_wait(barrier, 3 + planes - 1 + 3 + far_n - 1)

    started = []

    def go(copy):
        copy.start()
        started.append(copy)

    halves = (1 - yhi, yhi)

    go(remote(g_ref.at[1 - core], gpair, gps.at[0], gpr.at[0], partner))

    def pair_out(reg, half, k):
        yh = halves[half]
        go(
            remote(
                tm_ref.at[reg * 4 + yh * 2 + 1 - core, rows(k)],
                pair.at[reg * 2 + half, rows(k)],
                ps.at[reg * 2 + half, k],
                pr.at[reg * 2 + half, k],
                partner,
            )
        )

    def pair_sum(reg, half, k):
        ref = pair.at[reg * 2 + half, rows(k)]
        remote(ref, ref, ps.at[reg * 2 + half, k], pr.at[reg * 2 + half, k], partner).wait_recv()
        mine = tm_ref[reg * 4 + halves[half] * 2 + core, rows(k), :]
        return mine.astype(F32) + pair[reg * 2 + half, rows(k), :].astype(F32)

    def z_out(half, k):
        for d in (0, 1):
            zsend[d * 2 + half, rows(k), :] = pair_sum(1 + d, half, k).astype(BF)
            go(
                remote(
                    zsend.at[d * 2 + half, rows(k)],
                    zgot.at[d * 2 + half, rows(k)],
                    zs.at[d * 2 + half, k],
                    zr.at[d * 2 + half, k],
                    (down, up)[d],
                )
            )

    def region_sum(half, k):
        value = pair_sum(0, half, k)
        for d in (0, 1):
            ref = zgot.at[d * 2 + half, rows(k)]
            remote(ref, ref, zs.at[d * 2 + half, k], zr.at[d * 2 + half, k], up).wait_recv()
            value = value + zgot[d * 2 + half, rows(k), :].astype(F32)
        return value

    def ydev(k):
        return yup if k < 2 else ydown

    def y_out(k):
        ysend[rows(k), :] = region_sum(0, k).astype(BF)
        go(remote(ysend.at[rows(k)], relay.at[rows(k)], ys.at[k], rr.at[k], ydev(k)))

    def relay_on(k):
        ref = relay.at[rows(k)]
        remote(ref, ref, ys.at[k], rr.at[k], yup).wait_recv()
        go(remote(ref, ygot.at[rows(k)], rs.at[k], yr.at[k], ydev(k)))

    def finish(k):
        value = region_sum(1, k) + own_ref[rows(k), :]
        ref = ygot.at[rows(k)]
        remote(ref, ref, rs.at[k], yr.at[k], yup).wait_recv()
        out_ref[rows(k), :] = value + ygot[rows(k), :].astype(F32)

    for k in ORDER:
        pair_out(1, 0, k)
        pair_out(2, 0, k)
    for k in ORDER:
        pair_out(0, 0, k)
    for k in ORDER:
        pair_out(1, 1, k)
        pair_out(2, 1, k)
    for k in ORDER:
        pair_out(0, 1, k)

    remote(gpair, gpair, gps.at[0], gpr.at[0], partner).wait_recv()
    total[...] = g_ref[core] + gpair[...]
    width = ROWS // planes

    def piece(p):
        return pl.ds(pl.multiple_of(p * width, width), width)

    def plane_copy(d):
        p = (flat + d) % planes
        return remote(total.at[piece(p)], plane.at[flat], pls.at[d], plr.at[d], plane_dev(p))

    @pl.loop(1, planes)
    def _(d):
        plane_copy(d).start()

    for k in ORDER:
        z_out(0, k)

    plane[flat] = total[piece(flat), :]

    @pl.loop(1, planes)
    def _(d):
        ref = plane.at[(flat + planes - d) % planes]
        remote(ref, ref, pls.at[d], plr.at[d], partner).wait_recv()

    summed = plane[0]
    for p in range(1, planes):
        summed = summed + plane[p]
    part[...] = summed.reshape(4, width // 4, 128)
    quad[q] = part[q]

    def quad_copy(d):
        other = (q + d) % 4
        return remote(part.at[other], quad.at[q], qs.at[d], qr.at[d], me.zto(h * 4 + other))

    for d in range(1, 4):
        quad_copy(d).start()
    z_out(1, 0)
    z_out(1, 2)
    for d in range(1, 4):
        ref = quad.at[(q + 4 - d) % 4]
        remote(ref, ref, qs.at[d], qr.at[d], partner).wait_recv()
    far[h] = quad[0] + quad[1] + quad[2] + quad[3]

    def far_copy(d):
        return remote(far.at[h], far.at[h], fs.at[d], fr.at[d], me.zto((h + d) % far_n * 4 + q))

    for d in range(1, far_n):
        far_copy(d).start()
    z_out(1, 1)
    z_out(1, 3)
    y_out(0)
    y_out(2)
    y_out(1)
    y_out(3)
    for d in range(1, far_n):
        ref = far.at[(h + far_n - d) % far_n]
        remote(ref, ref, fs.at[d], fr.at[d], partner).wait_recv()
    for d in range(1, 4):
        quad_copy(d).wait_send()
    summed = far[0]
    for j in range(1, far_n):
        summed = summed + far[j]
    mine = full.at[core, piece(flat)]
    tile = width // 4

    def inner(j):
        return full.at[core, pl.ds(pl.multiple_of(flat * width + j * tile, tile), tile)]

    full[core, pl.ds(pl.multiple_of(flat * width + q * tile, tile), tile), :] = summed

    def again_copy(d):
        return remote(inner(q), inner(q), aqs.at[d], aqr.at[d], me.zto(h * 4 + (q + d) % 4))

    for d in range(1, 4):
        again_copy(d).start()
    for k in ORDER:
        relay_on(k)
    for d in range(1, 4):
        ref = inner((q + 4 - d) % 4)
        remote(ref, ref, aqs.at[d], aqr.at[d], partner).wait_recv()

    def spread_copy(d):
        return remote(mine, mine, aps.at[d], apr.at[d], plane_dev((flat + d) % planes))

    @pl.loop(1, planes)
    def _(d):
        spread_copy(d).start()

    for k in ORDER:
        finish(k)

    @pl.loop(1, planes)
    def _(d):
        ref = full.at[core, piece((flat + planes - d) % planes)]
        remote(ref, ref, aps.at[d], apr.at[d], partner).wait_recv()

    last = remote(full.at[core], full.at[core], gfs.at[0], gfr.at[0], partner)
    last.start()
    remote(full.at[1 - core], full.at[1 - core], gfs.at[0], gfr.at[0], partner).wait_recv()
    for i, ref in enumerate((gs_ref, gn_ref)):
        for c in (0, 1):
            ref[:, c * 128 : (c + 1) * 128] = full[c, i * 256 : (i + 1) * 256, :]

    last.wait_send()
    for d in range(1, 4):
        again_copy(d).wait_send()
    for d in range(1, far_n):
        far_copy(d).wait_send()

    @pl.loop(1, planes)
    def _(d):
        plane_copy(d).wait_send()
        spread_copy(d).wait_send()

    for copy in started:
        copy.wait_send()


def reduce_all(nx, nz, terms, grads, own):
    planes, far_n = nx * 4, nz // 4
    width = ROWS // planes
    big = (6, NK)
    return pl.pallas_call(
        functools.partial(reduce_kernel, nx, nz),
        out_shape=(
            jax.ShapeDtypeStruct((256, 256), F32),
            jax.ShapeDtypeStruct((256, 256), F32),
            jax.ShapeDtypeStruct((ROWS, 256), F32),
        ),
        in_specs=[VM] * 3,
        out_specs=(VM,) * 3,
        scratch_shapes=[
            pltpu.VMEM((6, ROWS, 256), BF),
            pltpu.VMEM((4, ROWS, 256), BF),
            pltpu.VMEM((4, ROWS, 256), BF),
            pltpu.VMEM((ROWS, 256), BF),
            pltpu.VMEM((ROWS, 256), BF),
            pltpu.VMEM((ROWS, 256), BF),
            pltpu.VMEM((ROWS, 128), F32),
            pltpu.VMEM((ROWS, 128), F32),
            pltpu.VMEM((planes, width, 128), F32),
            pltpu.VMEM((4, width // 4, 128), F32),
            pltpu.VMEM((far_n, width // 4, 128), F32),
            pltpu.VMEM((4, width // 4, 128), F32),
            pltpu.VMEM((2, ROWS, 128), F32),
            DMA(big), DMA(big), DMA((4, NK)), DMA((4, NK)),
            DMA((NK,)), DMA((NK,)), DMA((NK,)), DMA((NK,)),
            DMA((1,)), DMA((1,)), DMA((planes,)), DMA((planes,)),
            DMA((4,)), DMA((4,)), DMA((far_n,)), DMA((far_n,)),
            DMA((4,)), DMA((4,)), DMA((planes,)), DMA((planes,)),
            DMA((1,)), DMA((1,)),
        ],
        compiler_params=pltpu.CompilerParams(
            collective_id=1, has_side_effects=True, vmem_limit_bytes=48 << 20
        ),
        name="reduce_all",
    )(terms.reshape(12, ROWS, 256), grads, own)


def solution(mesh):
    nx, nz = mesh.shape["row"] // 2, mesh.shape["col"]
    split = P(("row", "col", "rep"))

    def on_device(features, self_weight, neigh_weight, block_source, edge_weights, labels):
        table = gather(nx, nz, features)
        terms, grads, own = local(
            table, features, self_weight, neigh_weight, block_source, edge_weights, labels
        )
        return reduce_all(nx, nz, terms, grads, own)

    return jax.shard_map(
        on_device,
        mesh=mesh,
        in_specs=(split, P(), P(), split, split, split),
        out_specs=(P(), P(), split),
        check_vma=False,
    )
```

```python
import functools

import jax
import jax.numpy as jnp
from jax import lax
from jax.experimental import pallas as pl
from jax.experimental.pallas import tpu as pltpu
from jax.sharding import PartitionSpec as P

MESH = pl.DeviceIdType.MESH
BF = jnp.bfloat16
F32 = jnp.float32
BLOCK = 64
ROWS = 512
NK = 4
CH = ROWS // NK
ORDER = (0, 2, 1, 3)
DMA = pltpu.SemaphoreType.DMA
VM = pl.BlockSpec(memory_space=pltpu.VMEM)
SM = pl.BlockSpec(memory_space=pltpu.SMEM)


def remote(src, dst, ssem, rsem, dev):
    return pltpu.make_async_remote_copy(
        src_ref=src, dst_ref=dst, send_sem=ssem, recv_sem=rsem, device_id=dev, device_id_type=MESH
    )


class Place:
    def __init__(self, nx, nz):
        self.nx, self.nz = nx, nz
        row, self.z, self.rep = lax.axis_index("row"), lax.axis_index("col"), lax.axis_index("rep")
        self.x, self.ylo = row // 2, row % 2
        self.yhi, self.core = self.rep // 2, self.rep % 2
        self.y = self.yhi * 2 + self.ylo
        self.row = row

    def at(self, x, y, z, core):
        return {"row": x * 2 + y % 2, "col": z, "rep": (y // 2) * 2 + core}

    def partner(self):
        return self.at(self.x, self.y, self.z, 1 - self.core)

    def ystep(self, d):
        return self.at(self.x, (self.y + d) % 4, self.z, self.core)

    def zto(self, z):
        return self.at(self.x, self.y, z, self.core)

    def zstep(self, d):
        return self.zto((self.z + d) % self.nz)


def signal(devs):
    barrier = pltpu.get_barrier_semaphore()
    for dev in devs:
        pl.semaphore_signal(barrier, inc=1, device_id=dev, device_id_type=MESH)
    return barrier


def rows(k):
    return pl.ds(k * CH, CH)


def split(value):
    high = value.astype(BF)
    return high, (value - high.astype(F32)).astype(BF)


def dot(a, b, dims=((1,), (0,))):
    return lax.dot_general(a, b, (dims, ((), ())), preferred_element_type=F32)


def dot3(a, b, dims=((1,), (0,))):
    return dot(a[0], b[0], dims) + (dot(a[0], b[1], dims) + dot(a[1], b[0], dims))


TURN = ((0,), (0,))
LAST = ((1,), (1,))


def sorted_slots(src, sel_ref):
    keys = src.astype(F32)
    grid = jnp.concatenate(
        [jnp.broadcast_to(keys[b : b + 1, :], (8, 8)) for b in range(8)]
        + [jnp.full((64, 8), 96.0, F32)],
        axis=0,
    )
    pick = lax.broadcasted_iota(jnp.int32, (128, 8), 0) % 8 == lax.broadcasted_iota(jnp.int32, (128, 8), 1)
    col = jnp.broadcast_to(jnp.sum(jnp.where(pick, grid, 0.0), axis=1, keepdims=True), (128, 128))
    row_id = lax.broadcasted_iota(jnp.int32, (128, 128), 0).astype(F32)
    lane_id = lax.broadcasted_iota(jnp.int32, (128, 128), 1).astype(F32)
    unique = col * 128.0 + row_id
    rank = jnp.sum(jnp.where(unique.T < unique, 1.0, 0.0), axis=1, keepdims=True)
    place = jnp.where(rank == lane_id, 1.0, 0.0)
    perm = jnp.sum(place * row_id, axis=0, keepdims=True)
    key = jnp.sum(place * col, axis=0, keepdims=True)
    again = jnp.where((key == pltpu.roll(key, 1, 1)) & (lane_id[0:1, :] > 0.0), 1.0, 0.0)
    final = jnp.maximum(jnp.sum(jnp.where(col <= lane_id, 1.0, 0.0), axis=0, keepdims=True) - 1.0, 0.0)
    named = jnp.minimum(jnp.sum(jnp.where(col == lane_id, 1.0, 0.0), axis=0, keepdims=True), 1.0)
    sel_ref[...] = jnp.zeros((8, 128), jnp.int32)
    for i, value in enumerate((perm, again, final, named)):
        sel_ref[i : i + 1, :] = value.astype(jnp.int32)


def gather_kernel(
    nx, nz, f_hbm, ws_hbm, wn_hbm, src_hbm, ew_hbm, lab_hbm,
    t_ref, wide_ref, flip_ref, inv_ref, base_ref, hot_ref, ft_ref, w_ref, sel_ref,
    relay, f_ref, ws_ref, wn_ref, ew_ref, src_ref, lab_ref, ls, ps, pr, zs, zr, ys, yr, rs, rr,
):
    me = Place(nx, nz)
    partner = me.partner()
    up, down = me.zstep(1), me.zstep(nz - 1)
    yup, ydown = me.ystep(1), me.ystep(3)
    barrier = signal((partner, up, down, yup, ydown))
    loads = [
        pltpu.make_async_copy(a, b, ls.at[i])
        for i, (a, b) in enumerate(
            (
                (f_hbm, f_ref),
                (src_hbm, src_ref),
                (ew_hbm, ew_ref),
                (ws_hbm, ws_ref),
                (wn_hbm, wn_ref),
                (lab_hbm, lab_ref),
            )
        )
    ]
    for load in loads:
        load.start()
    rep = me.rep
    other = (1 - me.yhi) * 2 + me.core
    loads[0].wait()
    t_ref[rep] = f_ref[...].astype(BF)
    pl.semaphore_wait(barrier, 5)

    started = []

    def go(copy):
        copy.start()
        started.append(copy)

    def slot(m, mine, across):
        return (mine, across, 4 + mine, 8 + mine, 4 + across, 8 + across)[m]

    def to_partner(m, k):
        ref = t_ref.at[slot(m, rep, other), rows(k)]
        go(remote(ref, ref, ps.at[m, k], pr.at[m, k], partner))

    def from_partner(m, k):
        prep, pother = me.yhi * 2 + 1 - me.core, (1 - me.yhi) * 2 + 1 - me.core
        ref = t_ref.at[slot(m, prep, pother), rows(k)]
        remote(ref, ref, ps.at[m, k], pr.at[m, k], partner).wait_recv()

    def to_z(half, k):
        mine = (rep, other)[half]
        src = t_ref.at[mine, rows(k)]
        go(remote(src, t_ref.at[4 + mine, rows(k)], zs.at[0, half, k], zr.at[0, half, k], up))
        go(remote(src, t_ref.at[8 + mine, rows(k)], zs.at[1, half, k], zr.at[1, half, k], down))

    def z_arrived(half, k):
        mine = (rep, other)[half]
        for d in (0, 1):
            ref = t_ref.at[4 + 4 * d + mine, rows(k)]
            remote(ref, ref, zs.at[d, half, k], zr.at[d, half, k], up).wait_recv()
            to_partner(2 + 2 * half + d, k)

    def ydev(k):
        return yup if k < 2 else ydown

    def to_relay(k):
        go(remote(t_ref.at[rep, rows(k)], relay.at[rows(k)], ys.at[k], rr.at[k], ydev(k)))

    def relay_on(k):
        ref = relay.at[rows(k)]
        remote(ref, ref, ys.at[k], rr.at[k], yup).wait_recv()
        origin = (me.y + (3 if k < 2 else 1)) % 4
        dst = t_ref.at[(origin // 2) * 2 + me.core, rows(k)]
        go(remote(ref, dst, rs.at[k], yr.at[k], ydev(k)))

    def y_arrived(k):
        ref = t_ref.at[other, rows(k)]
        remote(ref, ref, rs.at[k], yr.at[k], yup).wait_recv()
        to_z(1, k)
        to_partner(1, k)

    def widen(first):
        ones = jnp.ones((8 * BLOCK, 256), BF)
        for b in range(first, first + 4):
            here = slice(b * BLOCK, (b + 1) * BLOCK)
            cat = jnp.concatenate([ew_ref[b, s].astype(F32) for s in range(8)], axis=1)
            flip_ref[b * 8 : b * 8 + 8] = cat.T.astype(BF).reshape(8, BLOCK, BLOCK)
            low = cat.astype(BF)
            wide_ref[here, :] = low
            inv_ref[here, :] = 1.0 / dot(low, ones)

    def own_logits():
        for i, ref in enumerate((wn_ref, ws_ref)):
            w_ref[2 * i], w_ref[2 * i + 1] = split(ref[...])
        base_ref[...] = dot3(split(f_ref[...]), (w_ref[2], w_ref[3]))

    def turned():
        ft_ref[0], ft_ref[1] = split(f_ref[...].T)

    def targets():
        label = jnp.broadcast_to(lab_ref[...].astype(F32), (256, ROWS)).T
        column = lax.broadcasted_iota(jnp.int32, (ROWS, 256), 1).astype(F32)
        hot_ref[...] = jnp.where(label == column, 1.0, 0.0)

    for k in ORDER:
        to_relay(k)
        to_z(0, k)
    for k in ORDER:
        to_partner(0, k)
    for load in loads[1:]:
        load.wait()
    sorted_slots(src_ref[...], sel_ref)
    relay_on(0)
    relay_on(2)
    widen(0)
    relay_on(1)
    relay_on(3)
    z_arrived(0, 0)
    z_arrived(0, 2)
    widen(4)
    y_arrived(0)
    y_arrived(2)
    z_arrived(0, 1)
    turned()
    y_arrived(1)
    y_arrived(3)
    own_logits()
    z_arrived(0, 3)
    targets()
    for k in ORDER:
        z_arrived(1, k)
    for m in range(6):
        for k in ORDER:
            from_partner(m, k)
    for copy in started:
        copy.wait_send()


def gather(nx, nz, features, self_weight, neigh_weight, block_source, edge_weights, labels):
    hbm = pl.BlockSpec(memory_space=pltpu.HBM)
    wide = jax.ShapeDtypeStruct((ROWS, 256), F32)
    return pl.pallas_call(
        functools.partial(gather_kernel, nx, nz),
        out_shape=(
            jax.ShapeDtypeStruct((12, ROWS, 256), BF),
            jax.ShapeDtypeStruct((ROWS, ROWS), BF),
            jax.ShapeDtypeStruct((64, BLOCK, BLOCK), BF),
            wide,
            wide,
            wide,
            jax.ShapeDtypeStruct((2, 256, ROWS), BF),
            jax.ShapeDtypeStruct((4, 256, 256), BF),
            jax.ShapeDtypeStruct((8, 128), jnp.int32),
        ),
        in_specs=[hbm] * 6,
        out_specs=(VM,) * 9,
        scratch_shapes=[
            pltpu.VMEM((ROWS, 256), BF),
            pltpu.VMEM((ROWS, 256), F32),
            pltpu.VMEM((256, 256), F32),
            pltpu.VMEM((256, 256), F32),
            pltpu.VMEM((8, 8, BLOCK, BLOCK), jnp.int32),
            pltpu.VMEM((8, 8), jnp.int32),
            pltpu.VMEM((1, ROWS), jnp.int32),
            DMA((6,)),
            DMA((6, NK)),
            DMA((6, NK)),
            DMA((2, 2, NK)),
            DMA((2, 2, NK)),
            DMA((NK,)),
            DMA((NK,)),
            DMA((NK,)),
            DMA((NK,)),
        ],
        compiler_params=pltpu.CompilerParams(
            collective_id=0, has_side_effects=True, vmem_limit_bytes=20 << 20
        ),
        name="gather_tables",
    )(
        *(
            pltpu.with_memory_space_constraint(value, pltpu.HBM)
            for value in (
                features, self_weight, neigh_weight, block_source, edge_weights, labels.reshape(1, ROWS)
            )
        )
    )


def main_kernel(
    nx, nz, src, sel, t_ref, wide_ref, flip_ref, inv_ref, base_ref, hot_ref, ft_ref, w_ref,
    gs_ref, gn_ref, out_ref,
    mean, resid, spread, run, done, tmsend, g,
    pair, zsend, zgot, ysend, relay, ygot, gpair, total, plane, two, far, part, full,
    ps, pr, zs, zr, ys, yr, rs, rr, gps, gpr, pls, plr, qs, qr, fs, fr, aqs, aqr, aps, apr, gfs, gfr,
):
    me = Place(nx, nz)
    partner = me.partner()
    core, yhi, z = me.core, me.yhi, me.z
    up, down = me.zstep(1), me.zstep(nz - 1)
    yup, ydown = me.ystep(1), me.ystep(3)
    flat = me.x * 4 + me.y
    q, h = z % 2, z // 2
    far_n = nz // 2
    planes = nx * 4
    beside = me.zto(2 * h + 1 - q)

    def plane_dev(p):
        return me.at(p // 4, p % 4, z, core)

    barrier = signal((partner, up, down))

    def others(body):
        @pl.loop(0, planes)
        def _(p):
            @pl.when(p != flat)
            def _():
                body(p)

    @others
    def _(p):
        pl.semaphore_signal(barrier, inc=1, device_id=plane_dev(p), device_id_type=MESH)

    for d in range(1, far_n):
        pl.semaphore_signal(barrier, inc=1, device_id=me.zto((h + d) % far_n * 2 + q), device_id_type=MESH)

    started = []

    def go(copy):
        copy.start()
        started.append(copy)

    for b in range(8):
        here = pl.ds(b * BLOCK, BLOCK)
        table = jnp.concatenate([t_ref[src[b, s]] for s in range(8)], axis=0)
        m = dot(wide_ref[here, :], table) * inv_ref[here, :]
        mean[0, here, :], mean[1, here, :] = split(m)
    wn, ws = (w_ref[0], w_ref[1]), (w_ref[2], w_ref[3])
    logits = base_ref[...] + dot3((mean[0], mean[1]), wn)
    resid[0], resid[1] = split(1.0 / (1.0 + jnp.exp(-logits)) - hot_ref[...])

    halves = (1 - yhi, yhi)

    def pair_grad(i):
        here = pl.ds(i * 256, 256)
        return remote(g.at[1 - core, here], gpair.at[here], gps.at[i], gpr.at[i], partner)

    def weight_grad(i):
        if i == 0:
            value = dot3((ft_ref[0], ft_ref[1]), (resid[0], resid[1]))
        else:
            value = dot3((mean[0], mean[1]), (resid[0], resid[1]), TURN)
        for c in (0, 1):
            g[c, i * 256 : (i + 1) * 256, :] = value[:, c * 128 : (c + 1) * 128]

    weight_grad(0)
    pl.semaphore_wait(barrier, 3 + planes - 1 + far_n - 1)
    pair_grad(0).start()
    weight_grad(1)
    pair_grad(1).start()

    def block_terms(reg, r, k):
        found = []
        for j in range(CH // BLOCK):
            t = reg * 32 + r * 8 + k * (CH // BLOCK) + j
            found.append(done[sel[2, t]].astype(F32) * sel[3, t].astype(F32))
        return jnp.concatenate(found, axis=0)

    def pair_out(reg, half, k):
        at = reg * 2 + half
        tmsend[at, rows(k), :] = block_terms(reg, halves[half] * 2 + 1 - core, k).astype(BF)
        go(
            remote(
                tmsend.at[at, rows(k)], pair.at[at, rows(k)], ps.at[at, k], pr.at[at, k], partner
            )
        )

    def pair_sum(reg, half, k):
        ref = pair.at[reg * 2 + half, rows(k)]
        mine = block_terms(reg, halves[half] * 2 + core, k)
        remote(ref, ref, ps.at[reg * 2 + half, k], pr.at[reg * 2 + half, k], partner).wait_recv()
        return mine + pair[reg * 2 + half, rows(k), :].astype(F32)

    def z_out(half, k):
        for d in (0, 1):
            zsend[d * 2 + half, rows(k), :] = pair_sum(1 + d, half, k).astype(BF)
            go(
                remote(
                    zsend.at[d * 2 + half, rows(k)],
                    zgot.at[d * 2 + half, rows(k)],
                    zs.at[d * 2 + half, k],
                    zr.at[d * 2 + half, k],
                    (down, up)[d],
                )
            )

    def region_sum(half, k):
        value = pair_sum(0, half, k)
        for d in (0, 1):
            ref = zgot.at[d * 2 + half, rows(k)]
            remote(ref, ref, zs.at[d * 2 + half, k], zr.at[d * 2 + half, k], up).wait_recv()
            value = value + zgot[d * 2 + half, rows(k), :].astype(F32)
        return value

    def ydev(k):
        return yup if k < 2 else ydown

    def y_out(k):
        ysend[rows(k), :] = region_sum(0, k).astype(BF)
        go(remote(ysend.at[rows(k)], relay.at[rows(k)], ys.at[k], rr.at[k], ydev(k)))

    def relay_on(k):
        ref = relay.at[rows(k)]
        remote(ref, ref, ys.at[k], rr.at[k], yup).wait_recv()
        go(remote(ref, ygot.at[rows(k)], rs.at[k], yr.at[k], ydev(k)))

    def finish(k):
        value = region_sum(1, k) + out_ref[rows(k), :]
        ref = ygot.at[rows(k)]
        remote(ref, ref, rs.at[k], yr.at[k], yup).wait_recv()
        out_ref[rows(k), :] = value + ygot[rows(k), :].astype(F32)

    value = dot3((resid[0], resid[1]), wn, LAST) * inv_ref[...]
    spread[...] = value.astype(BF).reshape(8, BLOCK, 256)

    width = ROWS // planes

    def piece(p):
        return pl.ds(pl.multiple_of(p * width, width), width)

    def plane_copy(p):
        return remote(total.at[piece(p)], plane.at[flat], pls.at[p], plr.at[flat], plane_dev(p))

    for i in (0, 1):
        here = pl.ds(i * 256, 256)
        pair_grad(i).wait_recv()
        total[here, :] = g[core, here, :] + gpair[here, :]

        @pl.loop(i * planes // 2, (i + 1) * planes // 2)
        def _(p):
            @pl.when(p != flat)
            def _():
                plane_copy(p).start()

    run[...] = jnp.zeros((BLOCK, 256), F32)

    @pl.loop(0, 64, unroll=4)
    def _(r):
        at = sel[0, r]
        value = dot(flip_ref[at], spread[at // 8]) + run[...] * sel[1, r].astype(F32)
        run[...] = value
        done[r] = value.astype(BF)

    for k in ORDER:
        pair_out(1, 0, k)
        pair_out(2, 0, k)
    for k in ORDER:
        pair_out(0, 0, k)
    for k in ORDER:
        pair_out(1, 1, k)
        pair_out(2, 1, k)
    for k in ORDER:
        pair_out(0, 1, k)

    plane[flat] = total[piece(flat), :]

    @others
    def _(p):
        remote(plane.at[p], plane.at[p], pls.at[p], plr.at[p], partner).wait_recv()

    summed = plane[0]
    for p in range(1, planes):
        summed = summed + plane[p]
    part[...] = summed.reshape(2, width // 2, 128)
    two_copy = remote(part.at[1 - q], two, qs.at[0], qr.at[0], beside)
    two_copy.start()
    z_out(0, 0)
    two_copy.wait_recv()
    far[h] = part[q] + two[...]

    def far_copy(d):
        return remote(far.at[h], far.at[h], fs.at[d], fr.at[d], me.zto((h + d) % far_n * 2 + q))

    for d in sorted(range(1, far_n), key=lambda d: -min(d, far_n - d)):
        far_copy(d).start()
    for k in ORDER[1:]:
        z_out(0, k)
    out_ref[...] = dot3((resid[0], resid[1]), ws, LAST)
    y_out(0)
    y_out(2)
    for d in range(1, far_n):
        ref = far.at[(h + far_n - d) % far_n]
        remote(ref, ref, fs.at[d], fr.at[d], partner).wait_recv()
    summed = far[0]
    for j in range(1, far_n):
        summed = summed + far[j]
    tile = width // 2

    def inner(j):
        return full.at[core, pl.ds(pl.multiple_of(flat * width + j * tile, tile), tile)]

    full[core, pl.ds(pl.multiple_of(flat * width + q * tile, tile), tile), :] = summed
    again_copy = remote(inner(q), inner(q), aqs.at[0], aqr.at[0], beside)
    again_copy.start()
    for k in ORDER:
        z_out(1, k)
    y_out(1)
    y_out(3)
    remote(inner(1 - q), inner(1 - q), aqs.at[0], aqr.at[0], partner).wait_recv()
    mine = full.at[core, piece(flat)]

    def spread_copy(p):
        return remote(mine, mine, aps.at[p], apr.at[flat], plane_dev(p))

    def last_copy(p):
        ref = full.at[core, piece(p)]
        return remote(ref, ref, gfs.at[p], gfr.at[p], partner)

    @others
    def _(p):
        spread_copy(p).start()

    last_copy(flat).start()
    for k in ORDER:
        relay_on(k)

    @others
    def _(p):
        ref = full.at[core, piece(p)]
        remote(ref, ref, aps.at[p], apr.at[p], partner).wait_recv()
        last_copy(p).start()

    for k in ORDER:
        finish(k)

    @pl.loop(0, planes)
    def _(p):
        ref = full.at[1 - core, piece(p)]
        remote(ref, ref, gfs.at[p], gfr.at[p], partner).wait_recv()

    for i, ref in enumerate((gs_ref, gn_ref)):
        for c in (0, 1):
            ref[:, c * 128 : (c + 1) * 128] = full[c, i * 256 : (i + 1) * 256, :]

    for i in (0, 1):
        pair_grad(i).wait_send()
    two_copy.wait_send()
    again_copy.wait_send()
    for d in range(1, far_n):
        far_copy(d).wait_send()

    @others
    def _(p):
        plane_copy(p).wait_send()
        spread_copy(p).wait_send()

    @pl.loop(0, planes)
    def _(p):
        last_copy(p).wait_send()

    for copy in started:
        copy.wait_send()


def main(nx, nz, block_source, table, wide, flip, inv, base, hot, turned, weights, sel):
    planes, far_n = nx * 4, nz // 2
    width = ROWS // planes
    big = (6, NK)
    return pl.pallas_call(
        functools.partial(main_kernel, nx, nz),
        out_shape=(
            jax.ShapeDtypeStruct((256, 256), F32),
            jax.ShapeDtypeStruct((256, 256), F32),
            jax.ShapeDtypeStruct((ROWS, 256), F32),
        ),
        in_specs=[SM, SM] + [VM] * 8,
        out_specs=(VM,) * 3,
        scratch_shapes=[
            pltpu.VMEM((2, ROWS, 256), BF),
            pltpu.VMEM((2, ROWS, 256), BF),
            pltpu.VMEM((8, BLOCK, 256), BF),
            pltpu.VMEM((BLOCK, 256), F32),
            pltpu.VMEM((64, BLOCK, 256), BF),
            pltpu.VMEM((6, ROWS, 256), BF),
            pltpu.VMEM((2, ROWS, 128), F32),
            pltpu.VMEM((6, ROWS, 256), BF),
            pltpu.VMEM((4, ROWS, 256), BF),
            pltpu.VMEM((4, ROWS, 256), BF),
            pltpu.VMEM((ROWS, 256), BF),
            pltpu.VMEM((ROWS, 256), BF),
            pltpu.VMEM((ROWS, 256), BF),
            pltpu.VMEM((ROWS, 128), F32),
            pltpu.VMEM((ROWS, 128), F32),
            pltpu.VMEM((planes, width, 128), F32),
            pltpu.VMEM((width // 2, 128), F32),
            pltpu.VMEM((far_n, width // 2, 128), F32),
            pltpu.VMEM((2, width // 2, 128), F32),
            pltpu.VMEM((2, ROWS, 128), F32),
            DMA(big), DMA(big), DMA((4, NK)), DMA((4, NK)),
            DMA((NK,)), DMA((NK,)), DMA((NK,)), DMA((NK,)),
            DMA((2,)), DMA((2,)), DMA((planes,)), DMA((planes,)),
            DMA((1,)), DMA((1,)), DMA((far_n,)), DMA((far_n,)),
            DMA((1,)), DMA((1,)), DMA((planes,)), DMA((planes,)),
            DMA((planes,)), DMA((planes,)),
        ],
        compiler_params=pltpu.CompilerParams(
            collective_id=1, has_side_effects=True, vmem_limit_bytes=30 << 20
        ),
        name="main_math",
    )(block_source, sel, table.reshape(96, BLOCK, 256), wide, flip, inv, base, hot, turned, weights)


def store_kernel(a, b, c, a_hbm, b_hbm, c_hbm, sems):
    copies = [
        pltpu.make_async_copy(src, dst, sems.at[i])
        for i, (src, dst) in enumerate(((c, c_hbm), (a, a_hbm), (b, b_hbm)))
    ]
    for copy in copies:
        copy.start()
    for copy in copies:
        copy.wait()


def store(*values):
    return pl.pallas_call(
        store_kernel,
        out_shape=tuple(jax.ShapeDtypeStruct(v.shape, v.dtype) for v in values),
        in_specs=[VM] * 3,
        out_specs=(pl.BlockSpec(memory_space=pltpu.HBM),) * 3,
        scratch_shapes=[DMA((3,))],
        compiler_params=pltpu.CompilerParams(vmem_limit_bytes=8 << 20),
        name="store_results",
    )(*values)


def solution(mesh):
    nx, nz = mesh.shape["row"] // 2, mesh.shape["col"]
    split_rows = P(("row", "col", "rep"))

    def on_device(features, self_weight, neigh_weight, block_source, edge_weights, labels):
        prepared = gather(
            nx, nz, features, self_weight, neigh_weight, block_source, edge_weights, labels
        )
        return store(*main(nx, nz, block_source, *prepared))

    return jax.shard_map(
        on_device,
        mesh=mesh,
        in_specs=(split_rows, P(), P(), split_rows, split_rows, split_rows),
        out_specs=(P(), P(), split_rows),
        check_vma=False,
    )
```

```python
import functools

import jax
import jax.numpy as jnp
from jax import lax
from jax.experimental import pallas as pl
from jax.experimental.pallas import tpu as pltpu
from jax.sharding import PartitionSpec as P

MESH = pl.DeviceIdType.MESH
BF = jnp.bfloat16
F32 = jnp.float32
BLOCK = 64
ROWS = 512
NK = 4
CH = ROWS // NK
ORDER = (0, 2, 1, 3)
DMA = pltpu.SemaphoreType.DMA
REG = pltpu.SemaphoreType.REGULAR
VM = pl.BlockSpec(memory_space=pltpu.VMEM)
SM = pl.BlockSpec(memory_space=pltpu.SMEM)


def remote(src, dst, ssem, rsem, dev):
    return pltpu.make_async_remote_copy(
        src_ref=src, dst_ref=dst, send_sem=ssem, recv_sem=rsem, device_id=dev, device_id_type=MESH
    )


class Place:
    def __init__(self, nx, nz):
        self.nx, self.nz = nx, nz
        row, self.z, self.rep = lax.axis_index("row"), lax.axis_index("col"), lax.axis_index("rep")
        self.x, self.ylo = row // 2, row % 2
        self.yhi, self.core = self.rep // 2, self.rep % 2
        self.y = self.yhi * 2 + self.ylo
        self.row = row

    def at(self, x, y, z, core):
        return {"row": x * 2 + y % 2, "col": z, "rep": (y // 2) * 2 + core}

    def partner(self):
        return self.at(self.x, self.y, self.z, 1 - self.core)

    def ystep(self, d):
        return self.at(self.x, (self.y + d) % 4, self.z, self.core)

    def zto(self, z):
        return self.at(self.x, self.y, z, self.core)

    def zstep(self, d):
        return self.zto((self.z + d) % self.nz)


def signal(devs):
    barrier = pltpu.get_barrier_semaphore()
    for dev in devs:
        pl.semaphore_signal(barrier, inc=1, device_id=dev, device_id_type=MESH)
    return barrier


def rows(k):
    return pl.ds(k * CH, CH)


def split(value):
    high = value.astype(BF)
    return high, (value - high.astype(F32)).astype(BF)


def dot(a, b, dims=((1,), (0,))):
    return lax.dot_general(a, b, (dims, ((), ())), preferred_element_type=F32)


def dot3(a, b, dims=((1,), (0,))):
    return dot(a[0], b[0], dims) + (dot(a[0], b[1], dims) + dot(a[1], b[0], dims))


TURN = ((0,), (0,))
LAST = ((1,), (1,))


def sorted_slots(src, sel_ref):
    keys = src.astype(F32)
    grid = jnp.concatenate(
        [jnp.broadcast_to(keys[b : b + 1, :], (8, 8)) for b in range(8)]
        + [jnp.full((64, 8), 96.0, F32)],
        axis=0,
    )
    pick = lax.broadcasted_iota(jnp.int32, (128, 8), 0) % 8 == lax.broadcasted_iota(jnp.int32, (128, 8), 1)
    col = jnp.broadcast_to(jnp.sum(jnp.where(pick, grid, 0.0), axis=1, keepdims=True), (128, 128))
    row_id = lax.broadcasted_iota(jnp.int32, (128, 128), 0).astype(F32)
    lane_id = lax.broadcasted_iota(jnp.int32, (128, 128), 1).astype(F32)
    unique = col * 128.0 + row_id
    rank = jnp.sum(jnp.where(unique.T < unique, 1.0, 0.0), axis=1, keepdims=True)
    place = jnp.where(rank == lane_id, 1.0, 0.0)
    perm = jnp.sum(place * row_id, axis=0, keepdims=True)
    key = jnp.sum(place * col, axis=0, keepdims=True)
    again = jnp.where((key == pltpu.roll(key, 1, 1)) & (lane_id[0:1, :] > 0.0), 1.0, 0.0)
    final = jnp.maximum(jnp.sum(jnp.where(col <= lane_id, 1.0, 0.0), axis=0, keepdims=True) - 1.0, 0.0)
    named = jnp.minimum(jnp.sum(jnp.where(col == lane_id, 1.0, 0.0), axis=0, keepdims=True), 1.0)
    sel_ref[...] = jnp.zeros((8, 128), jnp.int32)
    for i, value in enumerate((perm, again, final, named)):
        sel_ref[i : i + 1, :] = value.astype(jnp.int32)


def gather_kernel(
    nx, nz, f_hbm, ws_hbm, wn_hbm, src_hbm, ew_hbm, lab_hbm,
    t_ref, wide_ref, flip_ref, inv_ref, base_ref, hot_ref, ft_ref, w_ref, sel_ref,
    relay, f_ref, ws_ref, wn_ref, ew_ref, src_ref, lab_ref, ls, ps, pr, zs, zr, ys, yr, rs, rr,
):
    me = Place(nx, nz)
    partner = me.partner()
    up, down = me.zstep(1), me.zstep(nz - 1)
    yup, ydown = me.ystep(1), me.ystep(3)
    barrier = signal((partner, up, down, yup, ydown))
    loads = [
        pltpu.make_async_copy(a, b, ls.at[i])
        for i, (a, b) in enumerate(
            (
                (f_hbm, f_ref),
                (src_hbm, src_ref),
                (ew_hbm, ew_ref),
                (ws_hbm, ws_ref),
                (wn_hbm, wn_ref),
                (lab_hbm, lab_ref),
            )
        )
    ]
    for load in loads:
        load.start()
    rep = me.rep
    other = (1 - me.yhi) * 2 + me.core
    loads[0].wait()
    t_ref[rep] = f_ref[...].astype(BF)
    pl.semaphore_wait(barrier, 5)

    started = []

    def go(copy):
        copy.start()
        started.append(copy)

    def slot(m, mine, across):
        return (mine, across, 4 + mine, 8 + mine, 4 + across, 8 + across)[m]

    def to_partner(m, k):
        ref = t_ref.at[slot(m, rep, other), rows(k)]
        go(remote(ref, ref, ps.at[m, k], pr.at[m, k], partner))

    def from_partner(m, k):
        prep, pother = me.yhi * 2 + 1 - me.core, (1 - me.yhi) * 2 + 1 - me.core
        ref = t_ref.at[slot(m, prep, pother), rows(k)]
        remote(ref, ref, ps.at[m, k], pr.at[m, k], partner).wait_recv()

    def to_z(half, k):
        mine = (rep, other)[half]
        src = t_ref.at[mine, rows(k)]
        go(remote(src, t_ref.at[4 + mine, rows(k)], zs.at[0, half, k], zr.at[0, half, k], up))
        go(remote(src, t_ref.at[8 + mine, rows(k)], zs.at[1, half, k], zr.at[1, half, k], down))

    def z_arrived(half, k):
        mine = (rep, other)[half]
        for d in (0, 1):
            ref = t_ref.at[4 + 4 * d + mine, rows(k)]
            remote(ref, ref, zs.at[d, half, k], zr.at[d, half, k], up).wait_recv()
            to_partner(2 + 2 * half + d, k)

    def ydev(k):
        return yup if k < 2 else ydown

    def to_relay(k):
        go(remote(t_ref.at[rep, rows(k)], relay.at[rows(k)], ys.at[k], rr.at[k], ydev(k)))

    def relay_on(k):
        ref = relay.at[rows(k)]
        remote(ref, ref, ys.at[k], rr.at[k], yup).wait_recv()
        origin = (me.y + (3 if k < 2 else 1)) % 4
        dst = t_ref.at[(origin // 2) * 2 + me.core, rows(k)]
        go(remote(ref, dst, rs.at[k], yr.at[k], ydev(k)))

    def y_arrived(k):
        ref = t_ref.at[other, rows(k)]
        remote(ref, ref, rs.at[k], yr.at[k], yup).wait_recv()
        to_z(1, k)
        to_partner(1, k)

    def widen(first):
        ones = jnp.ones((8 * BLOCK, 256), BF)
        for b in range(first, first + 4):
            here = slice(b * BLOCK, (b + 1) * BLOCK)
            cat = jnp.concatenate([ew_ref[b, s].astype(F32) for s in range(8)], axis=1)
            flip_ref[b * 8 : b * 8 + 8] = cat.T.astype(BF).reshape(8, BLOCK, BLOCK)
            low = cat.astype(BF)
            wide_ref[here, :] = low
            inv_ref[here, :] = 1.0 / dot(low, ones)

    def own_logits():
        for i, ref in enumerate((wn_ref, ws_ref)):
            w_ref[2 * i], w_ref[2 * i + 1] = split(ref[...])
        base_ref[...] = dot3(split(f_ref[...]), (w_ref[2], w_ref[3]))

    def turned():
        ft_ref[0], ft_ref[1] = split(f_ref[...].T)

    def targets():
        label = jnp.broadcast_to(lab_ref[...].astype(F32), (256, ROWS)).T
        column = lax.broadcasted_iota(jnp.int32, (ROWS, 256), 1).astype(F32)
        hot_ref[...] = jnp.where(label == column, 1.0, 0.0)

    for k in ORDER:
        to_relay(k)
        to_z(0, k)
    for k in ORDER:
        to_partner(0, k)
    for load in loads[1:]:
        load.wait()
    sorted_slots(src_ref[...], sel_ref)
    relay_on(0)
    relay_on(2)
    widen(0)
    relay_on(1)
    relay_on(3)
    z_arrived(0, 0)
    z_arrived(0, 2)
    widen(4)
    y_arrived(0)
    y_arrived(2)
    z_arrived(0, 1)
    turned()
    y_arrived(1)
    y_arrived(3)
    own_logits()
    z_arrived(0, 3)
    targets()
    for k in ORDER:
        z_arrived(1, k)
    for m in range(6):
        for k in ORDER:
            from_partner(m, k)
    for copy in started:
        copy.wait_send()


def gather(nx, nz, features, self_weight, neigh_weight, block_source, edge_weights, labels):
    hbm = pl.BlockSpec(memory_space=pltpu.HBM)
    wide = jax.ShapeDtypeStruct((ROWS, 256), F32)
    return pl.pallas_call(
        functools.partial(gather_kernel, nx, nz),
        out_shape=(
            jax.ShapeDtypeStruct((12, ROWS, 256), BF),
            jax.ShapeDtypeStruct((ROWS, ROWS), BF),
            jax.ShapeDtypeStruct((64, BLOCK, BLOCK), BF),
            wide,
            wide,
            wide,
            jax.ShapeDtypeStruct((2, 256, ROWS), BF),
            jax.ShapeDtypeStruct((4, 256, 256), BF),
            jax.ShapeDtypeStruct((8, 128), jnp.int32),
        ),
        in_specs=[hbm] * 6,
        out_specs=(VM,) * 9,
        scratch_shapes=[
            pltpu.VMEM((ROWS, 256), BF),
            pltpu.VMEM((ROWS, 256), F32),
            pltpu.VMEM((256, 256), F32),
            pltpu.VMEM((256, 256), F32),
            pltpu.VMEM((8, 8, BLOCK, BLOCK), jnp.int32),
            pltpu.VMEM((8, 8), jnp.int32),
            pltpu.VMEM((1, ROWS), jnp.int32),
            DMA((6,)),
            DMA((6, NK)),
            DMA((6, NK)),
            DMA((2, 2, NK)),
            DMA((2, 2, NK)),
            DMA((NK,)),
            DMA((NK,)),
            DMA((NK,)),
            DMA((NK,)),
        ],
        compiler_params=pltpu.CompilerParams(
            collective_id=0, has_side_effects=True, vmem_limit_bytes=20 << 20
        ),
        name="gather_tables",
    )(
        *(
            pltpu.with_memory_space_constraint(value, pltpu.HBM)
            for value in (
                features, self_weight, neigh_weight, block_source, edge_weights, labels.reshape(1, ROWS)
            )
        )
    )


def main_kernel(
    nx, nz, src, sel, t_ref, wide_ref, flip_ref, inv_ref, base_ref, hot_ref, ft_ref, w_ref,
    gs_ref, gn_ref, out_ref,
    mean, resid, spread, run, done, tmsend, g,
    pair, zsend, zgot, ysend, relay, ygot, gpair, total, plane, two, far, part, full,
    ps, pr, zs, zr, ys, yr, rs, rr, gps, gpr, pls, plr, qs, qr, fs, fr, aqs, aqr, aps, apr, gfs, gfr, word, zword,
):
    me = Place(nx, nz)
    partner = me.partner()
    core, yhi, z = me.core, me.yhi, me.z
    up, down = me.zstep(1), me.zstep(nz - 1)
    yup, ydown = me.ystep(1), me.ystep(3)
    flat = me.x * 4 + me.y
    q, h = z % 2, z // 2
    far_n = nz // 2
    planes = nx * 4
    beside = me.zto(2 * h + 1 - q)

    def plane_dev(p):
        return me.at(p // 4, p % 4, z, core)

    left, right = me.at((me.x + nx - 1) % nx, me.y, z, core), me.at((me.x + 1) % nx, me.y, z, core)
    barrier = signal((partner, up, down, yup, ydown, left, right))

    def others(body):
        @pl.loop(0, planes)
        def _(p):
            @pl.when(p != flat)
            def _():
                body(p)

    def tell(sem, devs):
        for dev in devs:
            pl.semaphore_signal(sem, inc=1, device_id=dev, device_id_type=MESH)

    def hear(sem):
        pl.semaphore_wait(sem, 2)

    started = []

    def go(copy):
        copy.start()
        started.append(copy)

    for b in range(8):
        here = pl.ds(b * BLOCK, BLOCK)
        table = jnp.concatenate([t_ref[src[b, s]] for s in range(8)], axis=0)
        m = dot(wide_ref[here, :], table) * inv_ref[here, :]
        mean[0, here, :], mean[1, here, :] = split(m)
    wn, ws = (w_ref[0], w_ref[1]), (w_ref[2], w_ref[3])
    logits = base_ref[...] + dot3((mean[0], mean[1]), wn)
    resid[0], resid[1] = split(1.0 / (1.0 + jnp.exp(-logits)) - hot_ref[...])

    halves = (1 - yhi, yhi)

    def pair_grad(i):
        here = pl.ds(i * 256, 256)
        return remote(g.at[1 - core, here], gpair.at[here], gps.at[i], gpr.at[i], partner)

    def weight_grad(i):
        if i == 0:
            value = dot3((ft_ref[0], ft_ref[1]), (resid[0], resid[1]))
        else:
            value = dot3((mean[0], mean[1]), (resid[0], resid[1]), TURN)
        for c in (0, 1):
            g[c, i * 256 : (i + 1) * 256, :] = value[:, c * 128 : (c + 1) * 128]

    pl.semaphore_wait(barrier, 7)
    tell(word.at[0], (left, right))
    tell(zword.at[0], (up, down))
    weight_grad(0)
    pair_grad(0).start()
    hear(word.at[0])
    tell(word.at[1], (yup, ydown))
    hear(zword.at[0])
    tell(zword.at[1], (up, down))
    weight_grad(1)
    pair_grad(1).start()
    hear(word.at[1])
    tell(word.at[2], (yup, ydown))
    hear(zword.at[1])
    tell(zword.at[2], (up, down))

    def block_terms(reg, r, k):
        found = []
        for j in range(CH // BLOCK):
            t = reg * 32 + r * 8 + k * (CH // BLOCK) + j
            found.append(done[sel[2, t]].astype(F32) * sel[3, t].astype(F32))
        return jnp.concatenate(found, axis=0)

    def pair_out(reg, half, k):
        at = reg * 2 + half
        tmsend[at, rows(k), :] = block_terms(reg, halves[half] * 2 + 1 - core, k).astype(BF)
        go(
            remote(
                tmsend.at[at, rows(k)], pair.at[at, rows(k)], ps.at[at, k], pr.at[at, k], partner
            )
        )

    def pair_sum(reg, half, k):
        ref = pair.at[reg * 2 + half, rows(k)]
        mine = block_terms(reg, halves[half] * 2 + core, k)
        remote(ref, ref, ps.at[reg * 2 + half, k], pr.at[reg * 2 + half, k], partner).wait_recv()
        return mine + pair[reg * 2 + half, rows(k), :].astype(F32)

    def z_out(half, k):
        for d in (0, 1):
            zsend[d * 2 + half, rows(k), :] = pair_sum(1 + d, half, k).astype(BF)
            go(
                remote(
                    zsend.at[d * 2 + half, rows(k)],
                    zgot.at[d * 2 + half, rows(k)],
                    zs.at[d * 2 + half, k],
                    zr.at[d * 2 + half, k],
                    (down, up)[d],
                )
            )

    def region_sum(half, k):
        value = pair_sum(0, half, k)
        for d in (0, 1):
            ref = zgot.at[d * 2 + half, rows(k)]
            remote(ref, ref, zs.at[d * 2 + half, k], zr.at[d * 2 + half, k], up).wait_recv()
            value = value + zgot[d * 2 + half, rows(k), :].astype(F32)
        return value

    def ydev(k):
        return yup if k < 2 else ydown

    def y_out(k):
        ysend[rows(k), :] = region_sum(0, k).astype(BF)
        go(remote(ysend.at[rows(k)], relay.at[rows(k)], ys.at[k], rr.at[k], ydev(k)))

    def relay_on(k):
        ref = relay.at[rows(k)]
        remote(ref, ref, ys.at[k], rr.at[k], yup).wait_recv()
        go(remote(ref, ygot.at[rows(k)], rs.at[k], yr.at[k], ydev(k)))

    def finish(k):
        value = region_sum(1, k) + out_ref[rows(k), :]
        ref = ygot.at[rows(k)]
        remote(ref, ref, rs.at[k], yr.at[k], yup).wait_recv()
        out_ref[rows(k), :] = value + ygot[rows(k), :].astype(F32)

    value = dot3((resid[0], resid[1]), wn, LAST) * inv_ref[...]
    spread[...] = value.astype(BF).reshape(8, BLOCK, 256)

    width = ROWS // planes

    def piece(p):
        return pl.ds(pl.multiple_of(p * width, width), width)

    def plane_copy(p):
        return remote(total.at[piece(p)], plane.at[flat], pls.at[p], plr.at[flat], plane_dev(p))

    hear(zword.at[2])
    tell(zword.at[3], (up, down))
    hear(word.at[2])
    for i in (0, 1):
        here = pl.ds(i * 256, 256)
        pair_grad(i).wait_recv()
        total[here, :] = (g[core, here, :] + gpair[here, :]).astype(BF)

        @pl.loop(i * planes // 2, (i + 1) * planes // 2)
        def _(p):
            @pl.when(p != flat)
            def _():
                plane_copy(p).start()

    hear(zword.at[3])
    tell(zword.at[4], (up, down))

    run[...] = jnp.zeros((BLOCK, 256), F32)

    @pl.loop(0, 64, unroll=4)
    def _(r):
        at = sel[0, r]
        value = dot(flip_ref[at], spread[at // 8]) + run[...] * sel[1, r].astype(F32)
        run[...] = value
        done[r] = value.astype(BF)

    hear(zword.at[4])
    tell(zword.at[5], (up, down))
    for k in ORDER:
        pair_out(1, 0, k)
        pair_out(2, 0, k)
    for k in ORDER:
        pair_out(0, 0, k)
    for k in ORDER:
        pair_out(1, 1, k)
        pair_out(2, 1, k)
    for k in ORDER:
        pair_out(0, 1, k)
    hear(zword.at[5])
    tell(zword.at[6], (up, down))

    plane[flat] = total[piece(flat), :]

    @others
    def _(p):
        remote(plane.at[p], plane.at[p], pls.at[p], plr.at[p], partner).wait_recv()

    summed = plane[0].astype(F32)
    for p in range(1, planes):
        summed = summed + plane[p].astype(F32)
    part[...] = summed.reshape(2, width // 2, 128)
    two_copy = remote(part.at[1 - q], two, qs.at[0], qr.at[0], beside)
    two_copy.start()
    hear(zword.at[6])
    z_out(0, 0)
    two_copy.wait_recv()
    far[h] = (part[q] + two[...]).astype(BF)

    def far_copy(d):
        return remote(far.at[h], far.at[h], fs.at[d], fr.at[d], me.zto((h + d) % far_n * 2 + q))

    for d in sorted(range(1, far_n), key=lambda d: -min(d, far_n - d)):
        far_copy(d).start()
    for k in ORDER[1:]:
        z_out(0, k)
    out_ref[...] = dot3((resid[0], resid[1]), ws, LAST)
    y_out(0)
    y_out(2)
    for d in range(1, far_n):
        ref = far.at[(h + far_n - d) % far_n]
        remote(ref, ref, fs.at[d], fr.at[d], partner).wait_recv()
    summed = far[0].astype(F32)
    for j in range(1, far_n):
        summed = summed + far[j].astype(F32)
    tile = width // 2

    def inner(j):
        return full.at[core, pl.ds(pl.multiple_of(flat * width + j * tile, tile), tile)]

    full[core, pl.ds(pl.multiple_of(flat * width + q * tile, tile), tile), :] = summed.astype(BF)
    again_copy = remote(inner(q), inner(q), aqs.at[0], aqr.at[0], beside)
    again_copy.start()
    for k in ORDER:
        z_out(1, k)
    y_out(1)
    y_out(3)
    remote(inner(1 - q), inner(1 - q), aqs.at[0], aqr.at[0], partner).wait_recv()
    mine = full.at[core, piece(flat)]

    def spread_copy(p):
        return remote(mine, mine, aps.at[p], apr.at[flat], plane_dev(p))

    def last_copy(p):
        ref = full.at[core, piece(p)]
        return remote(ref, ref, gfs.at[p], gfr.at[p], partner)

    @others
    def _(p):
        spread_copy(p).start()

    last_copy(flat).start()
    for k in ORDER:
        relay_on(k)

    @others
    def _(p):
        ref = full.at[core, piece(p)]
        remote(ref, ref, aps.at[p], apr.at[p], partner).wait_recv()
        last_copy(p).start()

    for k in ORDER:
        finish(k)

    @pl.loop(0, planes)
    def _(p):
        ref = full.at[1 - core, piece(p)]
        remote(ref, ref, gfs.at[p], gfr.at[p], partner).wait_recv()

    for i, ref in enumerate((gs_ref, gn_ref)):
        for c in (0, 1):
            ref[:, c * 128 : (c + 1) * 128] = full[c, i * 256 : (i + 1) * 256, :].astype(F32)

    for i in (0, 1):
        pair_grad(i).wait_send()
    two_copy.wait_send()
    again_copy.wait_send()
    for d in range(1, far_n):
        far_copy(d).wait_send()

    @others
    def _(p):
        plane_copy(p).wait_send()
        spread_copy(p).wait_send()

    @pl.loop(0, planes)
    def _(p):
        last_copy(p).wait_send()

    for copy in started:
        copy.wait_send()


def main(nx, nz, block_source, table, wide, flip, inv, base, hot, turned, weights, sel):
    planes, far_n = nx * 4, nz // 2
    width = ROWS // planes
    big = (6, NK)
    return pl.pallas_call(
        functools.partial(main_kernel, nx, nz),
        out_shape=(
            jax.ShapeDtypeStruct((256, 256), F32),
            jax.ShapeDtypeStruct((256, 256), F32),
            jax.ShapeDtypeStruct((ROWS, 256), F32),
        ),
        in_specs=[SM, SM] + [VM] * 8,
        out_specs=(VM,) * 3,
        scratch_shapes=[
            pltpu.VMEM((2, ROWS, 256), BF),
            pltpu.VMEM((2, ROWS, 256), BF),
            pltpu.VMEM((8, BLOCK, 256), BF),
            pltpu.VMEM((BLOCK, 256), F32),
            pltpu.VMEM((64, BLOCK, 256), BF),
            pltpu.VMEM((6, ROWS, 256), BF),
            pltpu.VMEM((2, ROWS, 128), F32),
            pltpu.VMEM((6, ROWS, 256), BF),
            pltpu.VMEM((4, ROWS, 256), BF),
            pltpu.VMEM((4, ROWS, 256), BF),
            pltpu.VMEM((ROWS, 256), BF),
            pltpu.VMEM((ROWS, 256), BF),
            pltpu.VMEM((ROWS, 256), BF),
            pltpu.VMEM((ROWS, 128), F32),
            pltpu.VMEM((ROWS, 128), BF),
            pltpu.VMEM((planes, width, 128), BF),
            pltpu.VMEM((width // 2, 128), F32),
            pltpu.VMEM((far_n, width // 2, 128), BF),
            pltpu.VMEM((2, width // 2, 128), F32),
            pltpu.VMEM((2, ROWS, 128), BF),
            DMA(big), DMA(big), DMA((4, NK)), DMA((4, NK)),
            DMA((NK,)), DMA((NK,)), DMA((NK,)), DMA((NK,)),
            DMA((2,)), DMA((2,)), DMA((planes,)), DMA((planes,)),
            DMA((1,)), DMA((1,)), DMA((far_n,)), DMA((far_n,)),
            DMA((1,)), DMA((1,)), DMA((planes,)), DMA((planes,)),
            DMA((planes,)), DMA((planes,)),
            REG((3,)), REG((7,)),
        ],
        compiler_params=pltpu.CompilerParams(
            collective_id=1, has_side_effects=True, vmem_limit_bytes=30 << 20
        ),
        name="main_math",
    )(block_source, sel, table.reshape(96, BLOCK, 256), wide, flip, inv, base, hot, turned, weights)


def store_kernel(a, b, c, a_hbm, b_hbm, c_hbm, sems):
    copies = [
        pltpu.make_async_copy(src, dst, sems.at[i])
        for i, (src, dst) in enumerate(((c, c_hbm), (a, a_hbm), (b, b_hbm)))
    ]
    for copy in copies:
        copy.start()
    for copy in copies:
        copy.wait()


def store(*values):
    return pl.pallas_call(
        store_kernel,
        out_shape=tuple(jax.ShapeDtypeStruct(v.shape, v.dtype) for v in values),
        in_specs=[VM] * 3,
        out_specs=(pl.BlockSpec(memory_space=pltpu.HBM),) * 3,
        scratch_shapes=[DMA((3,))],
        compiler_params=pltpu.CompilerParams(vmem_limit_bytes=8 << 20),
        name="store_results",
    )(*values)


def solution(mesh):
    nx, nz = mesh.shape["row"] // 2, mesh.shape["col"]
    split_rows = P(("row", "col", "rep"))

    def on_device(features, self_weight, neigh_weight, block_source, edge_weights, labels):
        prepared = gather(
            nx, nz, features, self_weight, neigh_weight, block_source, edge_weights, labels
        )
        return store(*main(nx, nz, block_source, *prepared))

    return jax.shard_map(
        on_device,
        mesh=mesh,
        in_specs=(split_rows, P(), P(), split_rows, split_rows, split_rows),
        out_specs=(P(), P(), split_rows),
        check_vma=False,
    )
```

```python
import functools

import jax
import jax.numpy as jnp
from jax import lax
from jax.experimental import pallas as pl
from jax.experimental.pallas import tpu as pltpu
from jax.sharding import PartitionSpec as P

MESH = pl.DeviceIdType.MESH
BF = jnp.bfloat16
F32 = jnp.float32
BLOCK = 64
ROWS = 512
NK = 4
CH = ROWS // NK
ORDER = (0, 2, 1, 3)
DMA = pltpu.SemaphoreType.DMA
VM = pl.BlockSpec(memory_space=pltpu.VMEM)
SM = pl.BlockSpec(memory_space=pltpu.SMEM)


def remote(src, dst, ssem, rsem, dev):
    return pltpu.make_async_remote_copy(
        src_ref=src, dst_ref=dst, send_sem=ssem, recv_sem=rsem, device_id=dev, device_id_type=MESH
    )


class Place:
    def __init__(self, nx, nz):
        self.nx, self.nz = nx, nz
        row, self.z, self.rep = lax.axis_index("row"), lax.axis_index("col"), lax.axis_index("rep")
        self.x, self.ylo = row // 2, row % 2
        self.yhi, self.core = self.rep // 2, self.rep % 2
        self.y = self.yhi * 2 + self.ylo
        self.row = row

    def at(self, x, y, z, core):
        return {"row": x * 2 + y % 2, "col": z, "rep": (y // 2) * 2 + core}

    def partner(self):
        return self.at(self.x, self.y, self.z, 1 - self.core)

    def ystep(self, d):
        return self.at(self.x, (self.y + d) % 4, self.z, self.core)

    def zto(self, z):
        return self.at(self.x, self.y, z, self.core)

    def zstep(self, d):
        return self.zto((self.z + d) % self.nz)


def signal(devs):
    barrier = pltpu.get_barrier_semaphore()
    for dev in devs:
        pl.semaphore_signal(barrier, inc=1, device_id=dev, device_id_type=MESH)
    return barrier


def rows(k):
    return pl.ds(k * CH, CH)


def split(value):
    high = value.astype(BF)
    return high, (value - high.astype(F32)).astype(BF)


def dot(a, b, dims=((1,), (0,))):
    return lax.dot_general(a, b, (dims, ((), ())), preferred_element_type=F32)


def dot3(a, b, dims=((1,), (0,))):
    return dot(a[0], b[0], dims) + (dot(a[0], b[1], dims) + dot(a[1], b[0], dims))


TURN = ((0,), (0,))
LAST = ((1,), (1,))


def sorted_slots(src, sel_ref):
    keys = src.astype(F32)
    grid = jnp.concatenate(
        [jnp.broadcast_to(keys[b : b + 1, :], (8, 8)) for b in range(8)]
        + [jnp.full((64, 8), 96.0, F32)],
        axis=0,
    )
    pick = lax.broadcasted_iota(jnp.int32, (128, 8), 0) % 8 == lax.broadcasted_iota(jnp.int32, (128, 8), 1)
    col = jnp.broadcast_to(jnp.sum(jnp.where(pick, grid, 0.0), axis=1, keepdims=True), (128, 128))
    row_id = lax.broadcasted_iota(jnp.int32, (128, 128), 0).astype(F32)
    lane_id = lax.broadcasted_iota(jnp.int32, (128, 128), 1).astype(F32)
    unique = col * 128.0 + row_id
    rank = jnp.sum(jnp.where(unique.T < unique, 1.0, 0.0), axis=1, keepdims=True)
    place = jnp.where(rank == lane_id, 1.0, 0.0)
    perm = jnp.sum(place * row_id, axis=0, keepdims=True)
    key = jnp.sum(place * col, axis=0, keepdims=True)
    again = jnp.where((key == pltpu.roll(key, 1, 1)) & (lane_id[0:1, :] > 0.0), 1.0, 0.0)
    final = jnp.maximum(jnp.sum(jnp.where(col <= lane_id, 1.0, 0.0), axis=0, keepdims=True) - 1.0, 0.0)
    named = jnp.minimum(jnp.sum(jnp.where(col == lane_id, 1.0, 0.0), axis=0, keepdims=True), 1.0)
    sel_ref[...] = jnp.zeros((8, 128), jnp.int32)
    for i, value in enumerate((perm, again, final, named)):
        sel_ref[i : i + 1, :] = value.astype(jnp.int32)


def gather_kernel(
    nx, nz, f_hbm, ws_hbm, wn_hbm, src_hbm, ew_hbm, lab_hbm,
    t_ref, wide_ref, flip_ref, inv_ref, base_ref, hot_ref, ft_ref, w_ref, sel_ref,
    relay, f_ref, ws_ref, wn_ref, ew_ref, src_ref, lab_ref, ls, ps, pr, zs, zr, ys, yr, rs, rr,
):
    me = Place(nx, nz)
    partner = me.partner()
    up, down = me.zstep(1), me.zstep(nz - 1)
    yup, ydown = me.ystep(1), me.ystep(3)
    barrier = signal((partner, up, down, yup, ydown))
    loads = [
        pltpu.make_async_copy(a, b, ls.at[i])
        for i, (a, b) in enumerate(
            (
                (f_hbm, f_ref),
                (src_hbm, src_ref),
                (ew_hbm, ew_ref),
                (ws_hbm, ws_ref),
                (wn_hbm, wn_ref),
                (lab_hbm, lab_ref),
            )
        )
    ]
    for load in loads:
        load.start()
    rep = me.rep
    other = (1 - me.yhi) * 2 + me.core
    loads[0].wait()
    t_ref[rep] = f_ref[...].astype(BF)
    pl.semaphore_wait(barrier, 5)

    started = []

    def go(copy):
        copy.start()
        started.append(copy)

    def slot(m, mine, across):
        return (mine, across, 4 + mine, 8 + mine, 4 + across, 8 + across)[m]

    def to_partner(m, k):
        ref = t_ref.at[slot(m, rep, other), rows(k)]
        go(remote(ref, ref, ps.at[m, k], pr.at[m, k], partner))

    def from_partner(m, k):
        prep, pother = me.yhi * 2 + 1 - me.core, (1 - me.yhi) * 2 + 1 - me.core
        ref = t_ref.at[slot(m, prep, pother), rows(k)]
        remote(ref, ref, ps.at[m, k], pr.at[m, k], partner).wait_recv()

    def to_z(half, k):
        mine = (rep, other)[half]
        src = t_ref.at[mine, rows(k)]
        go(remote(src, t_ref.at[4 + mine, rows(k)], zs.at[0, half, k], zr.at[0, half, k], up))
        go(remote(src, t_ref.at[8 + mine, rows(k)], zs.at[1, half, k], zr.at[1, half, k], down))

    def z_arrived(half, k):
        mine = (rep, other)[half]
        for d in (0, 1):
            ref = t_ref.at[4 + 4 * d + mine, rows(k)]
            remote(ref, ref, zs.at[d, half, k], zr.at[d, half, k], up).wait_recv()
            to_partner(2 + 2 * half + d, k)

    def ydev(k):
        return yup if k < 2 else ydown

    def to_relay(k):
        go(remote(t_ref.at[rep, rows(k)], relay.at[rows(k)], ys.at[k], rr.at[k], ydev(k)))

    def relay_on(k):
        ref = relay.at[rows(k)]
        remote(ref, ref, ys.at[k], rr.at[k], yup).wait_recv()
        origin = (me.y + (3 if k < 2 else 1)) % 4
        dst = t_ref.at[(origin // 2) * 2 + me.core, rows(k)]
        go(remote(ref, dst, rs.at[k], yr.at[k], ydev(k)))

    def y_arrived(k):
        ref = t_ref.at[other, rows(k)]
        remote(ref, ref, rs.at[k], yr.at[k], yup).wait_recv()
        to_z(1, k)
        to_partner(1, k)

    def widen(first):
        ones = jnp.ones((8 * BLOCK, 256), BF)
        for b in range(first, first + 4):
            here = slice(b * BLOCK, (b + 1) * BLOCK)
            cat = jnp.concatenate([ew_ref[b, s].astype(F32) for s in range(8)], axis=1)
            flip_ref[b * 8 : b * 8 + 8] = cat.T.astype(BF).reshape(8, BLOCK, BLOCK)
            low = cat.astype(BF)
            wide_ref[here, :] = low
            inv_ref[here, :] = 1.0 / dot(low, ones)

    def own_logits():
        for i, ref in enumerate((wn_ref, ws_ref)):
            w_ref[2 * i], w_ref[2 * i + 1] = split(ref[...])
        base_ref[...] = dot3(split(f_ref[...]), (w_ref[2], w_ref[3]))

    def turned():
        ft_ref[0], ft_ref[1] = split(f_ref[...].T)

    def targets():
        label = jnp.broadcast_to(lab_ref[...].astype(F32), (256, ROWS)).T
        column = lax.broadcasted_iota(jnp.int32, (ROWS, 256), 1).astype(F32)
        hot_ref[...] = jnp.where(label == column, 1.0, 0.0)

    for k in ORDER:
        to_relay(k)
        to_z(0, k)
    for k in ORDER:
        to_partner(0, k)
    for load in loads[1:]:
        load.wait()
    sorted_slots(src_ref[...], sel_ref)
    relay_on(0)
    relay_on(2)
    widen(0)
    relay_on(1)
    relay_on(3)
    z_arrived(0, 0)
    z_arrived(0, 2)
    widen(4)
    y_arrived(0)
    y_arrived(2)
    z_arrived(0, 1)
    turned()
    y_arrived(1)
    y_arrived(3)
    own_logits()
    z_arrived(0, 3)
    targets()
    for k in ORDER:
        z_arrived(1, k)
    for m in range(6):
        for k in ORDER:
            from_partner(m, k)
    for copy in started:
        copy.wait_send()


def gather(nx, nz, features, self_weight, neigh_weight, block_source, edge_weights, labels):
    hbm = pl.BlockSpec(memory_space=pltpu.HBM)
    wide = jax.ShapeDtypeStruct((ROWS, 256), F32)
    return pl.pallas_call(
        functools.partial(gather_kernel, nx, nz),
        out_shape=(
            jax.ShapeDtypeStruct((12, ROWS, 256), BF),
            jax.ShapeDtypeStruct((ROWS, ROWS), BF),
            jax.ShapeDtypeStruct((64, BLOCK, BLOCK), BF),
            wide,
            wide,
            wide,
            jax.ShapeDtypeStruct((2, 256, ROWS), BF),
            jax.ShapeDtypeStruct((4, 256, 256), BF),
            jax.ShapeDtypeStruct((8, 128), jnp.int32),
        ),
        in_specs=[hbm] * 6,
        out_specs=(VM,) * 9,
        scratch_shapes=[
            pltpu.VMEM((ROWS, 256), BF),
            pltpu.VMEM((ROWS, 256), F32),
            pltpu.VMEM((256, 256), F32),
            pltpu.VMEM((256, 256), F32),
            pltpu.VMEM((8, 8, BLOCK, BLOCK), jnp.int32),
            pltpu.VMEM((8, 8), jnp.int32),
            pltpu.VMEM((1, ROWS), jnp.int32),
            DMA((6,)),
            DMA((6, NK)),
            DMA((6, NK)),
            DMA((2, 2, NK)),
            DMA((2, 2, NK)),
            DMA((NK,)),
            DMA((NK,)),
            DMA((NK,)),
            DMA((NK,)),
        ],
        compiler_params=pltpu.CompilerParams(
            collective_id=0, has_side_effects=True, vmem_limit_bytes=20 << 20
        ),
        name="gather_tables",
    )(
        *(
            pltpu.with_memory_space_constraint(value, pltpu.HBM)
            for value in (
                features, self_weight, neigh_weight, block_source, edge_weights, labels.reshape(1, ROWS)
            )
        )
    )


def main_kernel(
    nx, nz, src, sel, t_ref, wide_ref, flip_ref, inv_ref, base_ref, hot_ref, ft_ref, w_ref,
    gs_ref, gn_ref, out_ref,
    mean, resid, spread, run, done, tmsend, g,
    pair, zsend, zgot, ysend, relay, ygot, gpair, total, plane, two, far, part, full,
    ps, pr, zs, zr, ys, yr, rs, rr, gps, gpr, pls, plr, qs, qr, fs, fr, aqs, aqr, aps, apr, gfs, gfr, word,
):
    me = Place(nx, nz)
    partner = me.partner()
    core, yhi, z = me.core, me.yhi, me.z
    up, down = me.zstep(1), me.zstep(nz - 1)
    yup, ydown = me.ystep(1), me.ystep(3)
    flat = me.x * 4 + me.y
    q, h = z % 2, z // 2
    far_n = nz // 2
    planes = nx * 4
    beside = me.zto(2 * h + 1 - q)

    def plane_dev(p):
        return me.at(p // 4, p % 4, z, core)

    steps = sorted(
        ((dx, dy) for dx in range(nx) for dy in range(4) if dx or dy),
        key=lambda s: -min(s[0], nx - s[0]) - min(s[1], 4 - s[1]),
    )

    def place(step):
        return (me.x + step[0]) % nx * 4 + (me.y + step[1]) % 4

    near = [me.zstep(d) for d in (1, nz - 1, 2, nz - 2, 4, nz - 4)]
    barrier = signal([plane_dev(place(step)) for step in steps] + near + [partner])

    def others(body):
        @pl.loop(0, planes)
        def _(p):
            @pl.when(p != flat)
            def _():
                body(p)

    started = []

    def go(copy):
        copy.start()
        started.append(copy)

    for b in range(8):
        here = pl.ds(b * BLOCK, BLOCK)
        table = jnp.concatenate([t_ref[src[b, s]] for s in range(8)], axis=0)
        m = dot(wide_ref[here, :], table) * inv_ref[here, :]
        mean[0, here, :], mean[1, here, :] = split(m)
    wn, ws = (w_ref[0], w_ref[1]), (w_ref[2], w_ref[3])
    logits = base_ref[...] + dot3((mean[0], mean[1]), wn)
    resid[0], resid[1] = split(1.0 / (1.0 + jnp.exp(-logits)) - hot_ref[...])

    halves = (1 - yhi, yhi)

    def pair_grad(i):
        here = pl.ds(i * 256, 256)
        return remote(g.at[1 - core, here], gpair.at[here], gps.at[i], gpr.at[i], partner)

    def weight_grad(i):
        if i == 0:
            value = dot3((ft_ref[0], ft_ref[1]), (resid[0], resid[1]))
        else:
            value = dot3((mean[0], mean[1]), (resid[0], resid[1]), TURN)
        for c in (0, 1):
            g[c, i * 256 : (i + 1) * 256, :] = value[:, c * 128 : (c + 1) * 128]

    weight_grad(0)
    pl.semaphore_wait(barrier, planes + len(near))
    pair_grad(0).start()
    for dev in near[4:]:
        pl.semaphore_signal(word, inc=1, device_id=dev, device_id_type=MESH)
    weight_grad(1)
    pair_grad(1).start()

    def block_terms(reg, r, k):
        found = []
        for j in range(CH // BLOCK):
            t = reg * 32 + r * 8 + k * (CH // BLOCK) + j
            found.append(done[sel[2, t]].astype(F32) * sel[3, t].astype(F32))
        return jnp.concatenate(found, axis=0)

    def pair_out(reg, half, k):
        at = reg * 2 + half
        tmsend[at, rows(k), :] = block_terms(reg, halves[half] * 2 + 1 - core, k).astype(BF)
        go(
            remote(
                tmsend.at[at, rows(k)], pair.at[at, rows(k)], ps.at[at, k], pr.at[at, k], partner
            )
        )

    def pair_sum(reg, half, k):
        ref = pair.at[reg * 2 + half, rows(k)]
        mine = block_terms(reg, halves[half] * 2 + core, k)
        remote(ref, ref, ps.at[reg * 2 + half, k], pr.at[reg * 2 + half, k], partner).wait_recv()
        return mine + pair[reg * 2 + half, rows(k), :].astype(F32)

    def z_out(half, k):
        for d in (0, 1):
            zsend[d * 2 + half, rows(k), :] = pair_sum(1 + d, half, k).astype(BF)
            go(
                remote(
                    zsend.at[d * 2 + half, rows(k)],
                    zgot.at[d * 2 + half, rows(k)],
                    zs.at[d * 2 + half, k],
                    zr.at[d * 2 + half, k],
                    (down, up)[d],
                )
            )

    def region_sum(half, k):
        value = pair_sum(0, half, k)
        for d in (0, 1):
            ref = zgot.at[d * 2 + half, rows(k)]
            remote(ref, ref, zs.at[d * 2 + half, k], zr.at[d * 2 + half, k], up).wait_recv()
            value = value + zgot[d * 2 + half, rows(k), :].astype(F32)
        return value

    def ydev(k):
        return yup if k < 2 else ydown

    def y_out(k):
        ysend[rows(k), :] = region_sum(0, k).astype(BF)
        go(remote(ysend.at[rows(k)], relay.at[rows(k)], ys.at[k], rr.at[k], ydev(k)))

    def relay_on(k):
        ref = relay.at[rows(k)]
        remote(ref, ref, ys.at[k], rr.at[k], yup).wait_recv()
        go(remote(ref, ygot.at[rows(k)], rs.at[k], yr.at[k], ydev(k)))

    def finish(k):
        value = region_sum(1, k) + out_ref[rows(k), :]
        ref = ygot.at[rows(k)]
        remote(ref, ref, rs.at[k], yr.at[k], yup).wait_recv()
        out_ref[rows(k), :] = value + ygot[rows(k), :].astype(F32)

    value = dot3((resid[0], resid[1]), wn, LAST) * inv_ref[...]
    spread[...] = value.astype(BF).reshape(8, BLOCK, 256)

    width = ROWS // planes

    def piece(p):
        return pl.ds(pl.multiple_of(p * width, width), width)

    def plane_copy(i):
        p = place(steps[i])
        return remote(total.at[piece(p)], plane.at[flat], pls.at[i], plr.at[flat], plane_dev(p))

    for i in (0, 1):
        here = pl.ds(i * 256, 256)
        pair_grad(i).wait_recv()
        total[here, :] = (g[core, here, :] + gpair[here, :]).astype(BF)

    for i in range(planes - 1):
        plane_copy(i).start()

    run[...] = jnp.zeros((BLOCK, 256), F32)

    @pl.loop(0, 64, unroll=4)
    def _(r):
        at = sel[0, r]
        value = dot(flip_ref[at], spread[at // 8]) + run[...] * sel[1, r].astype(F32)
        run[...] = value
        done[r] = value.astype(BF)

    for k in ORDER:
        pair_out(1, 0, k)
        pair_out(2, 0, k)
    for k in ORDER:
        pair_out(0, 0, k)
    for k in ORDER:
        pair_out(1, 1, k)
        pair_out(2, 1, k)
    for k in ORDER:
        pair_out(0, 1, k)

    plane[flat] = total[piece(flat), :]

    @others
    def _(p):
        remote(plane.at[p], plane.at[p], pls.at[p], plr.at[p], partner).wait_recv()

    summed = plane[0].astype(F32)
    for p in range(1, planes):
        summed = summed + plane[p].astype(F32)
    part[...] = summed.reshape(2, width // 2, 128)
    two_copy = remote(part.at[1 - q], two, qs.at[0], qr.at[0], beside)
    two_copy.start()
    z_out(0, 0)
    two_copy.wait_recv()
    far[h] = (part[q] + two[...]).astype(BF)

    def far_copy(d):
        return remote(far.at[h], far.at[h], fs.at[d], fr.at[d], me.zto((h + d) % far_n * 2 + q))

    pl.semaphore_wait(word, 2)
    for d in sorted(range(1, far_n), key=lambda d: -min(d, far_n - d)):
        far_copy(d).start()
    for k in ORDER[1:]:
        z_out(0, k)
    out_ref[...] = dot3((resid[0], resid[1]), ws, LAST)
    y_out(0)
    y_out(2)
    for d in range(1, far_n):
        ref = far.at[(h + far_n - d) % far_n]
        remote(ref, ref, fs.at[d], fr.at[d], partner).wait_recv()
    summed = far[0].astype(F32)
    for j in range(1, far_n):
        summed = summed + far[j].astype(F32)
    tile = width // 2

    def inner(j):
        return full.at[core, pl.ds(pl.multiple_of(flat * width + j * tile, tile), tile)]

    full[core, pl.ds(pl.multiple_of(flat * width + q * tile, tile), tile), :] = summed.astype(BF)
    again_copy = remote(inner(q), inner(q), aqs.at[0], aqr.at[0], beside)
    again_copy.start()
    for k in ORDER:
        z_out(1, k)
    y_out(1)
    y_out(3)
    remote(inner(1 - q), inner(1 - q), aqs.at[0], aqr.at[0], partner).wait_recv()
    mine = full.at[core, piece(flat)]

    def spread_copy(i):
        return remote(mine, mine, aps.at[i], apr.at[flat], plane_dev(place(steps[i])))

    def last_copy(p):
        ref = full.at[core, piece(p)]
        return remote(ref, ref, gfs.at[p], gfr.at[p], partner)

    for i in range(planes - 1):
        spread_copy(i).start()

    last_copy(flat).start()
    for k in ORDER:
        relay_on(k)

    @others
    def _(p):
        ref = full.at[core, piece(p)]
        remote(ref, ref, aps.at[p], apr.at[p], partner).wait_recv()
        last_copy(p).start()

    for k in ORDER:
        finish(k)

    @pl.loop(0, planes)
    def _(p):
        ref = full.at[1 - core, piece(p)]
        remote(ref, ref, gfs.at[p], gfr.at[p], partner).wait_recv()

    for i, ref in enumerate((gs_ref, gn_ref)):
        for c in (0, 1):
            ref[:, c * 128 : (c + 1) * 128] = full[c, i * 256 : (i + 1) * 256, :].astype(F32)

    for i in (0, 1):
        pair_grad(i).wait_send()
    two_copy.wait_send()
    again_copy.wait_send()
    for d in range(1, far_n):
        far_copy(d).wait_send()

    for i in range(planes - 1):
        plane_copy(i).wait_send()
        spread_copy(i).wait_send()

    @pl.loop(0, planes)
    def _(p):
        last_copy(p).wait_send()

    for copy in started:
        copy.wait_send()


def main(nx, nz, block_source, table, wide, flip, inv, base, hot, turned, weights, sel):
    planes, far_n = nx * 4, nz // 2
    width = ROWS // planes
    big = (6, NK)
    return pl.pallas_call(
        functools.partial(main_kernel, nx, nz),
        out_shape=(
            jax.ShapeDtypeStruct((256, 256), F32),
            jax.ShapeDtypeStruct((256, 256), F32),
            jax.ShapeDtypeStruct((ROWS, 256), F32),
        ),
        in_specs=[SM, SM] + [VM] * 8,
        out_specs=(VM,) * 3,
        scratch_shapes=[
            pltpu.VMEM((2, ROWS, 256), BF),
            pltpu.VMEM((2, ROWS, 256), BF),
            pltpu.VMEM((8, BLOCK, 256), BF),
            pltpu.VMEM((BLOCK, 256), F32),
            pltpu.VMEM((64, BLOCK, 256), BF),
            pltpu.VMEM((6, ROWS, 256), BF),
            pltpu.VMEM((2, ROWS, 128), F32),
            pltpu.VMEM((6, ROWS, 256), BF),
            pltpu.VMEM((4, ROWS, 256), BF),
            pltpu.VMEM((4, ROWS, 256), BF),
            pltpu.VMEM((ROWS, 256), BF),
            pltpu.VMEM((ROWS, 256), BF),
            pltpu.VMEM((ROWS, 256), BF),
            pltpu.VMEM((ROWS, 128), F32),
            pltpu.VMEM((ROWS, 128), BF),
            pltpu.VMEM((planes, width, 128), BF),
            pltpu.VMEM((width // 2, 128), F32),
            pltpu.VMEM((far_n, width // 2, 128), BF),
            pltpu.VMEM((2, width // 2, 128), F32),
            pltpu.VMEM((2, ROWS, 128), BF),
            DMA(big), DMA(big), DMA((4, NK)), DMA((4, NK)),
            DMA((NK,)), DMA((NK,)), DMA((NK,)), DMA((NK,)),
            DMA((2,)), DMA((2,)), DMA((planes,)), DMA((planes,)),
            DMA((1,)), DMA((1,)), DMA((far_n,)), DMA((far_n,)),
            DMA((1,)), DMA((1,)), DMA((planes,)), DMA((planes,)),
            DMA((planes,)), DMA((planes,)),
            pltpu.SemaphoreType.REGULAR,
        ],
        compiler_params=pltpu.CompilerParams(
            collective_id=1, has_side_effects=True, vmem_limit_bytes=30 << 20
        ),
        name="main_math",
    )(block_source, sel, table.reshape(96, BLOCK, 256), wide, flip, inv, base, hot, turned, weights)


def store_kernel(a, b, c, a_hbm, b_hbm, c_hbm, sems):
    copies = [
        pltpu.make_async_copy(src, dst, sems.at[i])
        for i, (src, dst) in enumerate(((c, c_hbm), (a, a_hbm), (b, b_hbm)))
    ]
    for copy in copies:
        copy.start()
    for copy in copies:
        copy.wait()


def store(*values):
    return pl.pallas_call(
        store_kernel,
        out_shape=tuple(jax.ShapeDtypeStruct(v.shape, v.dtype) for v in values),
        in_specs=[VM] * 3,
        out_specs=(pl.BlockSpec(memory_space=pltpu.HBM),) * 3,
        scratch_shapes=[DMA((3,))],
        compiler_params=pltpu.CompilerParams(vmem_limit_bytes=8 << 20),
        name="store_results",
    )(*values)


def solution(mesh):
    nx, nz = mesh.shape["row"] // 2, mesh.shape["col"]
    split_rows = P(("row", "col", "rep"))

    def on_device(features, self_weight, neigh_weight, block_source, edge_weights, labels):
        prepared = gather(
            nx, nz, features, self_weight, neigh_weight, block_source, edge_weights, labels
        )
        return store(*main(nx, nz, block_source, *prepared))

    return jax.shard_map(
        on_device,
        mesh=mesh,
        in_specs=(split_rows, P(), P(), split_rows, split_rows, split_rows),
        out_specs=(P(), P(), split_rows),
        check_vma=False,
    )
```

```python
import functools

import jax
import jax.numpy as jnp
from jax import lax
from jax.experimental import pallas as pl
from jax.experimental.pallas import tpu as pltpu
from jax.sharding import PartitionSpec as P

MESH = pl.DeviceIdType.MESH
BF = jnp.bfloat16
F32 = jnp.float32
BLOCK = 64
ROWS = 512
NK = 4
CH = ROWS // NK
ORDER = (0, 2, 1, 3)
DMA = pltpu.SemaphoreType.DMA
VM = pl.BlockSpec(memory_space=pltpu.VMEM)
SM = pl.BlockSpec(memory_space=pltpu.SMEM)


def remote(src, dst, ssem, rsem, dev):
    return pltpu.make_async_remote_copy(
        src_ref=src, dst_ref=dst, send_sem=ssem, recv_sem=rsem, device_id=dev, device_id_type=MESH
    )


class Place:
    def __init__(self, nx, nz):
        self.nx, self.nz = nx, nz
        row, self.z, self.rep = lax.axis_index("row"), lax.axis_index("col"), lax.axis_index("rep")
        self.x, self.ylo = row // 2, row % 2
        self.yhi, self.core = self.rep // 2, self.rep % 2
        self.y = self.yhi * 2 + self.ylo
        self.row = row

    def at(self, x, y, z, core):
        return {"row": x * 2 + y % 2, "col": z, "rep": (y // 2) * 2 + core}

    def partner(self):
        return self.at(self.x, self.y, self.z, 1 - self.core)

    def ystep(self, d):
        return self.at(self.x, (self.y + d) % 4, self.z, self.core)

    def zto(self, z):
        return self.at(self.x, self.y, z, self.core)

    def zstep(self, d):
        return self.zto((self.z + d) % self.nz)


def signal(devs):
    barrier = pltpu.get_barrier_semaphore()
    for dev in devs:
        pl.semaphore_signal(barrier, inc=1, device_id=dev, device_id_type=MESH)
    return barrier


def rows(k):
    return pl.ds(k * CH, CH)


def split(value):
    high = value.astype(BF)
    return high, (value - high.astype(F32)).astype(BF)


def dot(a, b, dims=((1,), (0,))):
    return lax.dot_general(a, b, (dims, ((), ())), preferred_element_type=F32)


def dot3(a, b, dims=((1,), (0,))):
    return dot(a[0], b[0], dims) + (dot(a[0], b[1], dims) + dot(a[1], b[0], dims))


TURN = ((0,), (0,))
LAST = ((1,), (1,))


def sorted_slots(src, sel_ref):
    keys = src.astype(F32)
    grid = jnp.concatenate(
        [jnp.broadcast_to(keys[b : b + 1, :], (8, 8)) for b in range(8)]
        + [jnp.full((64, 8), 96.0, F32)],
        axis=0,
    )
    pick = lax.broadcasted_iota(jnp.int32, (128, 8), 0) % 8 == lax.broadcasted_iota(jnp.int32, (128, 8), 1)
    col = jnp.broadcast_to(jnp.sum(jnp.where(pick, grid, 0.0), axis=1, keepdims=True), (128, 128))
    row_id = lax.broadcasted_iota(jnp.int32, (128, 128), 0).astype(F32)
    lane_id = lax.broadcasted_iota(jnp.int32, (128, 128), 1).astype(F32)
    unique = col * 128.0 + row_id
    rank = jnp.sum(jnp.where(unique.T < unique, 1.0, 0.0), axis=1, keepdims=True)
    place = jnp.where(rank == lane_id, 1.0, 0.0)
    perm = jnp.sum(place * row_id, axis=0, keepdims=True)
    key = jnp.sum(place * col, axis=0, keepdims=True)
    again = jnp.where((key == pltpu.roll(key, 1, 1)) & (lane_id[0:1, :] > 0.0), 1.0, 0.0)
    final = jnp.maximum(jnp.sum(jnp.where(col <= lane_id, 1.0, 0.0), axis=0, keepdims=True) - 1.0, 0.0)
    named = jnp.minimum(jnp.sum(jnp.where(col == lane_id, 1.0, 0.0), axis=0, keepdims=True), 1.0)
    sel_ref[...] = jnp.zeros((8, 128), jnp.int32)
    for i, value in enumerate((perm, again, final, named)):
        sel_ref[i : i + 1, :] = value.astype(jnp.int32)


def gather_kernel(
    nx, nz, f_hbm, ws_hbm, wn_hbm, src_hbm, ew_hbm, lab_hbm,
    t_ref, wide_ref, flip_ref, inv_ref, base_ref, hot_ref, ft_ref, w_ref, sel_ref,
    relay, f_ref, ws_ref, wn_ref, ew_ref, src_ref, lab_ref, ls, ps, pr, zs, zr, ys, yr, rs, rr,
):
    me = Place(nx, nz)
    partner = me.partner()
    up, down = me.zstep(1), me.zstep(nz - 1)
    yup, ydown = me.ystep(1), me.ystep(3)
    barrier = signal((partner, up, down, yup, ydown))
    loads = [
        pltpu.make_async_copy(a, b, ls.at[i])
        for i, (a, b) in enumerate(
            (
                (f_hbm, f_ref),
                (src_hbm, src_ref),
                (ew_hbm, ew_ref),
                (ws_hbm, ws_ref),
                (wn_hbm, wn_ref),
                (lab_hbm, lab_ref),
            )
        )
    ]
    for load in loads:
        load.start()
    rep = me.rep
    other = (1 - me.yhi) * 2 + me.core
    loads[0].wait()
    t_ref[rep] = f_ref[...].astype(BF)
    pl.semaphore_wait(barrier, 5)

    started = []

    def go(copy):
        copy.start()
        started.append(copy)

    def slot(m, mine, across):
        return (mine, across, 4 + mine, 8 + mine, 4 + across, 8 + across)[m]

    def to_partner(m, k):
        ref = t_ref.at[slot(m, rep, other), rows(k)]
        go(remote(ref, ref, ps.at[m, k], pr.at[m, k], partner))

    def from_partner(m, k):
        prep, pother = me.yhi * 2 + 1 - me.core, (1 - me.yhi) * 2 + 1 - me.core
        ref = t_ref.at[slot(m, prep, pother), rows(k)]
        remote(ref, ref, ps.at[m, k], pr.at[m, k], partner).wait_recv()

    def to_z(half, k):
        mine = (rep, other)[half]
        src = t_ref.at[mine, rows(k)]
        go(remote(src, t_ref.at[4 + mine, rows(k)], zs.at[0, half, k], zr.at[0, half, k], up))
        go(remote(src, t_ref.at[8 + mine, rows(k)], zs.at[1, half, k], zr.at[1, half, k], down))

    def z_arrived(half, k):
        mine = (rep, other)[half]
        for d in (0, 1):
            ref = t_ref.at[4 + 4 * d + mine, rows(k)]
            remote(ref, ref, zs.at[d, half, k], zr.at[d, half, k], up).wait_recv()
            to_partner(2 + 2 * half + d, k)

    def ydev(k):
        return yup if k < 2 else ydown

    def to_relay(k):
        go(remote(t_ref.at[rep, rows(k)], relay.at[rows(k)], ys.at[k], rr.at[k], ydev(k)))

    def relay_on(k):
        ref = relay.at[rows(k)]
        remote(ref, ref, ys.at[k], rr.at[k], yup).wait_recv()
        origin = (me.y + (3 if k < 2 else 1)) % 4
        dst = t_ref.at[(origin // 2) * 2 + me.core, rows(k)]
        go(remote(ref, dst, rs.at[k], yr.at[k], ydev(k)))

    def y_arrived(k):
        ref = t_ref.at[other, rows(k)]
        remote(ref, ref, rs.at[k], yr.at[k], yup).wait_recv()
        to_z(1, k)
        to_partner(1, k)

    def widen(first):
        ones = jnp.ones((8 * BLOCK, 256), BF)
        for b in range(first, first + 4):
            here = slice(b * BLOCK, (b + 1) * BLOCK)
            cat = jnp.concatenate([ew_ref[b, s].astype(F32) for s in range(8)], axis=1)
            flip_ref[b * 8 : b * 8 + 8] = cat.T.astype(BF).reshape(8, BLOCK, BLOCK)
            low = cat.astype(BF)
            wide_ref[here, :] = low
            inv_ref[here, :] = 1.0 / dot(low, ones)

    def own_logits():
        for i, ref in enumerate((wn_ref, ws_ref)):
            w_ref[2 * i], w_ref[2 * i + 1] = split(ref[...])
        base_ref[...] = dot3(split(f_ref[...]), (w_ref[2], w_ref[3]))

    def turned():
        ft_ref[0], ft_ref[1] = split(f_ref[...].T)

    def targets():
        label = jnp.broadcast_to(lab_ref[...].astype(F32), (256, ROWS)).T
        column = lax.broadcasted_iota(jnp.int32, (ROWS, 256), 1).astype(F32)
        hot_ref[...] = jnp.where(label == column, 1.0, 0.0)

    for k in ORDER:
        to_relay(k)
        to_z(0, k)
    for k in ORDER:
        to_partner(0, k)
    for load in loads[1:]:
        load.wait()
    sorted_slots(src_ref[...], sel_ref)
    relay_on(0)
    relay_on(2)
    widen(0)
    relay_on(1)
    relay_on(3)
    z_arrived(0, 0)
    z_arrived(0, 2)
    widen(4)
    y_arrived(0)
    y_arrived(2)
    z_arrived(0, 1)
    turned()
    y_arrived(1)
    y_arrived(3)
    own_logits()
    z_arrived(0, 3)
    targets()
    for k in ORDER:
        z_arrived(1, k)
    for m in range(6):
        for k in ORDER:
            from_partner(m, k)
    for copy in started:
        copy.wait_send()


def gather(nx, nz, features, self_weight, neigh_weight, block_source, edge_weights, labels):
    hbm = pl.BlockSpec(memory_space=pltpu.HBM)
    wide = jax.ShapeDtypeStruct((ROWS, 256), F32)
    return pl.pallas_call(
        functools.partial(gather_kernel, nx, nz),
        out_shape=(
            jax.ShapeDtypeStruct((12, ROWS, 256), BF),
            jax.ShapeDtypeStruct((ROWS, ROWS), BF),
            jax.ShapeDtypeStruct((64, BLOCK, BLOCK), BF),
            wide,
            wide,
            wide,
            jax.ShapeDtypeStruct((2, 256, ROWS), BF),
            jax.ShapeDtypeStruct((4, 256, 256), BF),
            jax.ShapeDtypeStruct((8, 128), jnp.int32),
        ),
        in_specs=[hbm] * 6,
        out_specs=(VM,) * 9,
        scratch_shapes=[
            pltpu.VMEM((ROWS, 256), BF),
            pltpu.VMEM((ROWS, 256), F32),
            pltpu.VMEM((256, 256), F32),
            pltpu.VMEM((256, 256), F32),
            pltpu.VMEM((8, 8, BLOCK, BLOCK), jnp.int32),
            pltpu.VMEM((8, 8), jnp.int32),
            pltpu.VMEM((1, ROWS), jnp.int32),
            DMA((6,)),
            DMA((6, NK)),
            DMA((6, NK)),
            DMA((2, 2, NK)),
            DMA((2, 2, NK)),
            DMA((NK,)),
            DMA((NK,)),
            DMA((NK,)),
            DMA((NK,)),
        ],
        compiler_params=pltpu.CompilerParams(
            collective_id=0, has_side_effects=True, vmem_limit_bytes=20 << 20
        ),
        name="gather_tables",
    )(
        *(
            pltpu.with_memory_space_constraint(value, pltpu.HBM)
            for value in (
                features, self_weight, neigh_weight, block_source, edge_weights, labels.reshape(1, ROWS)
            )
        )
    )


def main_kernel(
    nx, nz, src, sel, t_ref, wide_ref, flip_ref, inv_ref, base_ref, hot_ref, ft_ref, w_ref,
    gs_ref, gn_ref, out_ref,
    mean, resid, spread, run, done, tmsend, g,
    pair, zsend, zgot, ysend, relay, ygot, gpair, total, plane, two, far, part, full,
    ps, pr, zs, zr, ys, yr, rs, rr, gps, gpr, pls, plr, qs, qr, fs, fr, aps, apr, gfs, gfr, word,
):
    me = Place(nx, nz)
    partner = me.partner()
    core, yhi, z = me.core, me.yhi, me.z
    up, down = me.zstep(1), me.zstep(nz - 1)
    yup, ydown = me.ystep(1), me.ystep(3)
    flat = me.x * 4 + me.y
    q, h = z % 2, z // 2
    planes = nx * 4
    beside = me.zto(2 * h + 1 - q)

    def plane_dev(p):
        return me.at(p // 4, p % 4, z, core)

    steps = sorted(
        ((dx, dy) for dx in range(nx) for dy in range(4) if dx or dy),
        key=lambda s: -min(s[0], nx - s[0]) - min(s[1], 4 - s[1]),
    )

    def place(step):
        return (me.x + step[0]) % nx * 4 + (me.y + step[1]) % 4

    near = [me.zstep(d) for d in (1, nz - 1, 2, nz - 2, 3, nz - 3, 4, nz - 4)]
    barrier = signal([plane_dev(place(step)) for step in steps] + near + [partner])

    def others(body):
        @pl.loop(0, planes)
        def _(p):
            @pl.when(p != flat)
            def _():
                body(p)

    started = []

    def go(copy):
        copy.start()
        started.append(copy)

    for b in range(8):
        here = pl.ds(b * BLOCK, BLOCK)
        table = jnp.concatenate([t_ref[src[b, s]] for s in range(8)], axis=0)
        m = dot(wide_ref[here, :], table) * inv_ref[here, :]
        mean[0, here, :], mean[1, here, :] = split(m)
    wn, ws = (w_ref[0], w_ref[1]), (w_ref[2], w_ref[3])
    logits = base_ref[...] + dot3((mean[0], mean[1]), wn)
    resid[0], resid[1] = split(1.0 / (1.0 + jnp.exp(-logits)) - hot_ref[...])

    halves = (1 - yhi, yhi)

    def pair_grad(i):
        here = pl.ds(i * 256, 256)
        return remote(g.at[1 - core, here], gpair.at[here], gps.at[i], gpr.at[i], partner)

    def weight_grad(i):
        if i == 0:
            value = dot3((ft_ref[0], ft_ref[1]), (resid[0], resid[1]))
        else:
            value = dot3((mean[0], mean[1]), (resid[0], resid[1]), TURN)
        for c in (0, 1):
            g[c, i * 256 : (i + 1) * 256, :] = value[:, c * 128 : (c + 1) * 128]

    weight_grad(0)
    pl.semaphore_wait(barrier, planes + len(near))
    pair_grad(0).start()
    for dev in near[6:]:
        pl.semaphore_signal(word, inc=1, device_id=dev, device_id_type=MESH)
    weight_grad(1)
    pair_grad(1).start()

    def block_terms(reg, r, k):
        found = []
        for j in range(CH // BLOCK):
            t = reg * 32 + r * 8 + k * (CH // BLOCK) + j
            found.append(done[sel[2, t]].astype(F32) * sel[3, t].astype(F32))
        return jnp.concatenate(found, axis=0)

    def pair_out(reg, half, k):
        at = reg * 2 + half
        tmsend[at, rows(k), :] = block_terms(reg, halves[half] * 2 + 1 - core, k).astype(BF)
        go(
            remote(
                tmsend.at[at, rows(k)], pair.at[at, rows(k)], ps.at[at, k], pr.at[at, k], partner
            )
        )

    def pair_sum(reg, half, k):
        ref = pair.at[reg * 2 + half, rows(k)]
        mine = block_terms(reg, halves[half] * 2 + core, k)
        remote(ref, ref, ps.at[reg * 2 + half, k], pr.at[reg * 2 + half, k], partner).wait_recv()
        return mine + pair[reg * 2 + half, rows(k), :].astype(F32)

    def z_out(half, k):
        for d in (0, 1):
            zsend[d * 2 + half, rows(k), :] = pair_sum(1 + d, half, k).astype(BF)
            go(
                remote(
                    zsend.at[d * 2 + half, rows(k)],
                    zgot.at[d * 2 + half, rows(k)],
                    zs.at[d * 2 + half, k],
                    zr.at[d * 2 + half, k],
                    (down, up)[d],
                )
            )

    def region_sum(half, k):
        value = pair_sum(0, half, k)
        for d in (0, 1):
            ref = zgot.at[d * 2 + half, rows(k)]
            remote(ref, ref, zs.at[d * 2 + half, k], zr.at[d * 2 + half, k], up).wait_recv()
            value = value + zgot[d * 2 + half, rows(k), :].astype(F32)
        return value

    def ydev(k):
        return yup if k < 2 else ydown

    def y_out(k):
        ysend[rows(k), :] = region_sum(0, k).astype(BF)
        go(remote(ysend.at[rows(k)], relay.at[rows(k)], ys.at[k], rr.at[k], ydev(k)))

    def relay_on(k):
        ref = relay.at[rows(k)]
        remote(ref, ref, ys.at[k], rr.at[k], yup).wait_recv()
        go(remote(ref, ygot.at[rows(k)], rs.at[k], yr.at[k], ydev(k)))

    def finish(k):
        value = region_sum(1, k) + out_ref[rows(k), :]
        ref = ygot.at[rows(k)]
        remote(ref, ref, rs.at[k], yr.at[k], yup).wait_recv()
        out_ref[rows(k), :] = value + ygot[rows(k), :].astype(F32)

    width = ROWS // planes

    def piece(p):
        return pl.ds(pl.multiple_of(p * width, width), width)

    def plane_copy(i):
        p = place(steps[i])
        return remote(total.at[piece(p)], plane.at[flat], pls.at[i], plr.at[flat], plane_dev(p))

    def plane_out(i):
        here = pl.ds(i * 256, 256)
        pair_grad(i).wait_recv()
        total[here, :] = (g[core, here, :] + gpair[here, :]).astype(BF)
        for j in range(planes - 1):

            @pl.when(place(steps[j]) * 2 // planes == i)
            def _():
                plane_copy(j).start()

    plane_out(0)
    value = dot3((resid[0], resid[1]), wn, LAST) * inv_ref[...]
    spread[...] = value.astype(BF).reshape(8, BLOCK, 256)
    plane_out(1)

    run[...] = jnp.zeros((BLOCK, 256), F32)

    @pl.loop(0, 64, unroll=4)
    def _(r):
        at = sel[0, r]
        value = dot(flip_ref[at], spread[at // 8]) + run[...] * sel[1, r].astype(F32)
        run[...] = value
        done[r] = value.astype(BF)

    for k in ORDER:
        pair_out(1, 0, k)
        pair_out(2, 0, k)
    for k in ORDER:
        pair_out(0, 0, k)
    for k in ORDER:
        pair_out(1, 1, k)
        pair_out(2, 1, k)
    for k in ORDER:
        pair_out(0, 1, k)

    plane[flat] = total[piece(flat), :]

    @others
    def _(p):
        remote(plane.at[p], plane.at[p], pls.at[p], plr.at[p], partner).wait_recv()

    summed = plane[0].astype(F32)
    for p in range(1, planes):
        summed = summed + plane[p].astype(F32)
    part[...] = summed.reshape(2, width // 2, 128)
    two_copy = remote(part.at[1 - q], two, qs.at[0], qr.at[0], beside)
    two_copy.start()
    z_out(0, 0)
    two_copy.wait_recv()
    far[z] = (part[q] + two[...]).astype(BF)

    def far_copy(d):
        return remote(far.at[z], far.at[z], fs.at[d], fr.at[d], me.zstep(d))

    pl.semaphore_wait(word, 2)
    for d in sorted(range(1, nz), key=lambda d: -min(d, nz - d)):
        far_copy(d).start()
    for k in ORDER[1:]:
        z_out(0, k)
    out_ref[...] = dot3((resid[0], resid[1]), ws, LAST)
    y_out(0)
    y_out(2)
    for d in range(1, nz):
        ref = far.at[(z + nz - d) % nz]
        remote(ref, ref, fs.at[d], fr.at[d], partner).wait_recv()
    tile = width // 2
    for j in (0, 1):
        summed = far[j].astype(F32)
        for i in range(j + 2, nz, 2):
            summed = summed + far[i].astype(F32)
        here = pl.ds(pl.multiple_of(flat * width + j * tile, tile), tile)
        full[core, here, :] = summed.astype(BF)
    mine = full.at[core, piece(flat)]

    def spread_copy(i):
        return remote(mine, mine, aps.at[i], apr.at[flat], plane_dev(place(steps[i])))

    def last_copy(p):
        ref = full.at[core, piece(p)]
        return remote(ref, ref, gfs.at[p], gfr.at[p], partner)

    for i in range(planes - 1):
        spread_copy(i).start()
    last_copy(flat).start()
    for k in ORDER:
        z_out(1, k)
    y_out(1)
    y_out(3)
    for k in ORDER:
        relay_on(k)

    @others
    def _(p):
        ref = full.at[core, piece(p)]
        remote(ref, ref, aps.at[p], apr.at[p], partner).wait_recv()
        last_copy(p).start()

    for k in ORDER:
        finish(k)

    @pl.loop(0, planes)
    def _(p):
        ref = full.at[1 - core, piece(p)]
        remote(ref, ref, gfs.at[p], gfr.at[p], partner).wait_recv()

    for i, ref in enumerate((gs_ref, gn_ref)):
        for c in (0, 1):
            ref[:, c * 128 : (c + 1) * 128] = full[c, i * 256 : (i + 1) * 256, :].astype(F32)

    for i in (0, 1):
        pair_grad(i).wait_send()
    two_copy.wait_send()
    for d in range(1, nz):
        far_copy(d).wait_send()

    for i in range(planes - 1):
        plane_copy(i).wait_send()
        spread_copy(i).wait_send()

    @pl.loop(0, planes)
    def _(p):
        last_copy(p).wait_send()

    for copy in started:
        copy.wait_send()


def main(nx, nz, block_source, table, wide, flip, inv, base, hot, turned, weights, sel):
    planes = nx * 4
    width = ROWS // planes
    big = (6, NK)
    return pl.pallas_call(
        functools.partial(main_kernel, nx, nz),
        out_shape=(
            jax.ShapeDtypeStruct((256, 256), F32),
            jax.ShapeDtypeStruct((256, 256), F32),
            jax.ShapeDtypeStruct((ROWS, 256), F32),
        ),
        in_specs=[SM, SM] + [VM] * 8,
        out_specs=(VM,) * 3,
        scratch_shapes=[
            pltpu.VMEM((2, ROWS, 256), BF),
            pltpu.VMEM((2, ROWS, 256), BF),
            pltpu.VMEM((8, BLOCK, 256), BF),
            pltpu.VMEM((BLOCK, 256), F32),
            pltpu.VMEM((64, BLOCK, 256), BF),
            pltpu.VMEM((6, ROWS, 256), BF),
            pltpu.VMEM((2, ROWS, 128), F32),
            pltpu.VMEM((6, ROWS, 256), BF),
            pltpu.VMEM((4, ROWS, 256), BF),
            pltpu.VMEM((4, ROWS, 256), BF),
            pltpu.VMEM((ROWS, 256), BF),
            pltpu.VMEM((ROWS, 256), BF),
            pltpu.VMEM((ROWS, 256), BF),
            pltpu.VMEM((ROWS, 128), F32),
            pltpu.VMEM((ROWS, 128), BF),
            pltpu.VMEM((planes, width, 128), BF),
            pltpu.VMEM((width // 2, 128), F32),
            pltpu.VMEM((nz, width // 2, 128), BF),
            pltpu.VMEM((2, width // 2, 128), F32),
            pltpu.VMEM((2, ROWS, 128), BF),
            DMA(big), DMA(big), DMA((4, NK)), DMA((4, NK)),
            DMA((NK,)), DMA((NK,)), DMA((NK,)), DMA((NK,)),
            DMA((2,)), DMA((2,)), DMA((planes,)), DMA((planes,)),
            DMA((1,)), DMA((1,)), DMA((nz,)), DMA((nz,)),
            DMA((planes,)), DMA((planes,)),
            DMA((planes,)), DMA((planes,)),
            pltpu.SemaphoreType.REGULAR,
        ],
        compiler_params=pltpu.CompilerParams(
            collective_id=1, has_side_effects=True, vmem_limit_bytes=30 << 20
        ),
        name="main_math",
    )(block_source, sel, table.reshape(96, BLOCK, 256), wide, flip, inv, base, hot, turned, weights)


def store_kernel(a, b, c, a_hbm, b_hbm, c_hbm, sems):
    copies = [
        pltpu.make_async_copy(src, dst, sems.at[i])
        for i, (src, dst) in enumerate(((c, c_hbm), (a, a_hbm), (b, b_hbm)))
    ]
    for copy in copies:
        copy.start()
    for copy in copies:
        copy.wait()


def store(*values):
    return pl.pallas_call(
        store_kernel,
        out_shape=tuple(jax.ShapeDtypeStruct(v.shape, v.dtype) for v in values),
        in_specs=[VM] * 3,
        out_specs=(pl.BlockSpec(memory_space=pltpu.HBM),) * 3,
        scratch_shapes=[DMA((3,))],
        compiler_params=pltpu.CompilerParams(vmem_limit_bytes=8 << 20),
        name="store_results",
    )(*values)


def solution(mesh):
    nx, nz = mesh.shape["row"] // 2, mesh.shape["col"]
    split_rows = P(("row", "col", "rep"))

    def on_device(features, self_weight, neigh_weight, block_source, edge_weights, labels):
        prepared = gather(
            nx, nz, features, self_weight, neigh_weight, block_source, edge_weights, labels
        )
        return store(*main(nx, nz, block_source, *prepared))

    return jax.shard_map(
        on_device,
        mesh=mesh,
        in_specs=(split_rows, P(), P(), split_rows, split_rows, split_rows),
        out_specs=(P(), P(), split_rows),
        check_vma=False,
    )
```

```python
import functools

import jax
import jax.numpy as jnp
from jax import lax
from jax.experimental import pallas as pl
from jax.experimental.pallas import tpu as pltpu
from jax.sharding import PartitionSpec as P

MESH = pl.DeviceIdType.MESH
BF = jnp.bfloat16
F32 = jnp.float32
BLOCK = 64
ROWS = 512
NK = 4
CH = ROWS // NK
ORDER = (0, 2, 1, 3)
DMA = pltpu.SemaphoreType.DMA
VM = pl.BlockSpec(memory_space=pltpu.VMEM)
SM = pl.BlockSpec(memory_space=pltpu.SMEM)


def remote(src, dst, ssem, rsem, dev):
    return pltpu.make_async_remote_copy(
        src_ref=src, dst_ref=dst, send_sem=ssem, recv_sem=rsem, device_id=dev, device_id_type=MESH
    )


class Place:
    def __init__(self, nx, nz):
        self.nx, self.nz = nx, nz
        row, self.z, self.rep = lax.axis_index("row"), lax.axis_index("col"), lax.axis_index("rep")
        self.x, self.ylo = row // 2, row % 2
        self.yhi, self.core = self.rep // 2, self.rep % 2
        self.y = self.yhi * 2 + self.ylo
        self.row = row

    def at(self, x, y, z, core):
        return {"row": x * 2 + y % 2, "col": z, "rep": (y // 2) * 2 + core}

    def partner(self):
        return self.at(self.x, self.y, self.z, 1 - self.core)

    def ystep(self, d):
        return self.at(self.x, (self.y + d) % 4, self.z, self.core)

    def zto(self, z):
        return self.at(self.x, self.y, z, self.core)

    def zstep(self, d):
        return self.zto((self.z + d) % self.nz)


def signal(devs):
    barrier = pltpu.get_barrier_semaphore()
    for dev in devs:
        pl.semaphore_signal(barrier, inc=1, device_id=dev, device_id_type=MESH)
    return barrier


def rows(k):
    return pl.ds(k * CH, CH)


def split(value):
    high = value.astype(BF)
    return high, (value - high.astype(F32)).astype(BF)


def dot(a, b, dims=((1,), (0,))):
    return lax.dot_general(a, b, (dims, ((), ())), preferred_element_type=F32)


def dot3(a, b, dims=((1,), (0,))):
    return dot(a[0], b[0], dims) + (dot(a[0], b[1], dims) + dot(a[1], b[0], dims))


TURN = ((0,), (0,))
LAST = ((1,), (1,))


def sorted_slots(src, sel_ref):
    keys = src.astype(F32)
    grid = jnp.concatenate(
        [jnp.broadcast_to(keys[b : b + 1, :], (8, 8)) for b in range(8)]
        + [jnp.full((64, 8), 96.0, F32)],
        axis=0,
    )
    pick = lax.broadcasted_iota(jnp.int32, (128, 8), 0) % 8 == lax.broadcasted_iota(jnp.int32, (128, 8), 1)
    col = jnp.broadcast_to(jnp.sum(jnp.where(pick, grid, 0.0), axis=1, keepdims=True), (128, 128))
    row_id = lax.broadcasted_iota(jnp.int32, (128, 128), 0).astype(F32)
    lane_id = lax.broadcasted_iota(jnp.int32, (128, 128), 1).astype(F32)
    unique = col * 128.0 + row_id
    rank = jnp.sum(jnp.where(unique.T < unique, 1.0, 0.0), axis=1, keepdims=True)
    place = jnp.where(rank == lane_id, 1.0, 0.0)
    perm = jnp.sum(place * row_id, axis=0, keepdims=True)
    key = jnp.sum(place * col, axis=0, keepdims=True)
    again = jnp.where((key == pltpu.roll(key, 1, 1)) & (lane_id[0:1, :] > 0.0), 1.0, 0.0)
    final = jnp.maximum(jnp.sum(jnp.where(col <= lane_id, 1.0, 0.0), axis=0, keepdims=True) - 1.0, 0.0)
    named = jnp.minimum(jnp.sum(jnp.where(col == lane_id, 1.0, 0.0), axis=0, keepdims=True), 1.0)
    sel_ref[...] = jnp.zeros((8, 128), jnp.int32)
    for i, value in enumerate((perm, again, final, named)):
        sel_ref[i : i + 1, :] = value.astype(jnp.int32)


def gather_kernel(
    nx, nz, f_hbm, ws_hbm, wn_hbm, src_hbm, ew_hbm, lab_hbm,
    t_ref, wide_ref, flip_ref, inv_ref, base_ref, hot_ref, ft_ref, w_ref, sel_ref,
    relay, f_ref, ws_ref, wn_ref, ew_ref, src_ref, lab_ref, ls, ps, pr, zs, zr, ys, yr, rs, rr,
):
    me = Place(nx, nz)
    partner = me.partner()
    up, down = me.zstep(1), me.zstep(nz - 1)
    yup, ydown = me.ystep(1), me.ystep(3)
    barrier = signal((partner, up, down, yup, ydown))
    loads = [
        pltpu.make_async_copy(a, b, ls.at[i])
        for i, (a, b) in enumerate(
            (
                (f_hbm, f_ref),
                (src_hbm, src_ref),
                (ew_hbm, ew_ref),
                (ws_hbm, ws_ref),
                (wn_hbm, wn_ref),
                (lab_hbm, lab_ref),
            )
        )
    ]
    for load in loads:
        load.start()
    rep = me.rep
    other = (1 - me.yhi) * 2 + me.core
    loads[0].wait()
    t_ref[rep] = f_ref[...].astype(BF)
    pl.semaphore_wait(barrier, 5)

    started = []

    def go(copy):
        copy.start()
        started.append(copy)

    def slot(m, mine, across):
        return (mine, across, 4 + mine, 8 + mine, 4 + across, 8 + across)[m]

    def to_partner(m, k):
        ref = t_ref.at[slot(m, rep, other), rows(k)]
        go(remote(ref, ref, ps.at[m, k], pr.at[m, k], partner))

    def from_partner(m, k):
        prep, pother = me.yhi * 2 + 1 - me.core, (1 - me.yhi) * 2 + 1 - me.core
        ref = t_ref.at[slot(m, prep, pother), rows(k)]
        remote(ref, ref, ps.at[m, k], pr.at[m, k], partner).wait_recv()

    def to_z(half, k):
        mine = (rep, other)[half]
        src = t_ref.at[mine, rows(k)]
        go(remote(src, t_ref.at[4 + mine, rows(k)], zs.at[0, half, k], zr.at[0, half, k], up))
        go(remote(src, t_ref.at[8 + mine, rows(k)], zs.at[1, half, k], zr.at[1, half, k], down))

    def z_arrived(half, k):
        mine = (rep, other)[half]
        for d in (0, 1):
            ref = t_ref.at[4 + 4 * d + mine, rows(k)]
            remote(ref, ref, zs.at[d, half, k], zr.at[d, half, k], up).wait_recv()
            to_partner(2 + 2 * half + d, k)

    def ydev(k):
        return yup if k < 2 else ydown

    def to_relay(k):
        go(remote(t_ref.at[rep, rows(k)], relay.at[rows(k)], ys.at[k], rr.at[k], ydev(k)))

    def relay_on(k):
        ref = relay.at[rows(k)]
        remote(ref, ref, ys.at[k], rr.at[k], yup).wait_recv()
        origin = (me.y + (3 if k < 2 else 1)) % 4
        dst = t_ref.at[(origin // 2) * 2 + me.core, rows(k)]
        go(remote(ref, dst, rs.at[k], yr.at[k], ydev(k)))

    def y_arrived(k):
        ref = t_ref.at[other, rows(k)]
        remote(ref, ref, rs.at[k], yr.at[k], yup).wait_recv()
        to_z(1, k)
        to_partner(1, k)

    def widen(first):
        ones = jnp.ones((8 * BLOCK, 256), BF)
        for b in range(first, first + 4):
            here = slice(b * BLOCK, (b + 1) * BLOCK)
            cat = jnp.concatenate([ew_ref[b, s].astype(F32) for s in range(8)], axis=1)
            flip_ref[b * 8 : b * 8 + 8] = cat.T.astype(BF).reshape(8, BLOCK, BLOCK)
            low = cat.astype(BF)
            wide_ref[here, :] = low
            inv_ref[here, :] = 1.0 / dot(low, ones)

    def own_logits():
        for i, ref in enumerate((wn_ref, ws_ref)):
            w_ref[2 * i], w_ref[2 * i + 1] = split(ref[...])
        base_ref[...] = dot3(split(f_ref[...]), (w_ref[2], w_ref[3]))

    def turned():
        ft_ref[0], ft_ref[1] = split(f_ref[...].T)

    def targets():
        label = jnp.broadcast_to(lab_ref[...].astype(F32), (256, ROWS)).T
        column = lax.broadcasted_iota(jnp.int32, (ROWS, 256), 1).astype(F32)
        hot_ref[...] = jnp.where(label == column, 1.0, 0.0)

    for k in ORDER:
        to_relay(k)
        to_z(0, k)
    for k in ORDER:
        to_partner(0, k)
    for load in loads[1:]:
        load.wait()
    sorted_slots(src_ref[...], sel_ref)
    relay_on(0)
    relay_on(2)
    widen(0)
    relay_on(1)
    relay_on(3)
    z_arrived(0, 0)
    z_arrived(0, 2)
    widen(4)
    y_arrived(0)
    y_arrived(2)
    z_arrived(0, 1)
    turned()
    y_arrived(1)
    y_arrived(3)
    own_logits()
    z_arrived(0, 3)
    targets()
    for k in ORDER:
        z_arrived(1, k)
    for m in range(6):
        for k in ORDER:
            from_partner(m, k)
    for copy in started:
        copy.wait_send()


def gather(nx, nz, features, self_weight, neigh_weight, block_source, edge_weights, labels):
    hbm = pl.BlockSpec(memory_space=pltpu.HBM)
    wide = jax.ShapeDtypeStruct((ROWS, 256), F32)
    return pl.pallas_call(
        functools.partial(gather_kernel, nx, nz),
        out_shape=(
            jax.ShapeDtypeStruct((12, ROWS, 256), BF),
            jax.ShapeDtypeStruct((ROWS, ROWS), BF),
            jax.ShapeDtypeStruct((64, BLOCK, BLOCK), BF),
            wide,
            wide,
            wide,
            jax.ShapeDtypeStruct((2, 256, ROWS), BF),
            jax.ShapeDtypeStruct((4, 256, 256), BF),
            jax.ShapeDtypeStruct((8, 128), jnp.int32),
        ),
        in_specs=[hbm] * 6,
        out_specs=(VM,) * 9,
        scratch_shapes=[
            pltpu.VMEM((ROWS, 256), BF),
            pltpu.VMEM((ROWS, 256), F32),
            pltpu.VMEM((256, 256), F32),
            pltpu.VMEM((256, 256), F32),
            pltpu.VMEM((8, 8, BLOCK, BLOCK), jnp.int32),
            pltpu.VMEM((8, 8), jnp.int32),
            pltpu.VMEM((1, ROWS), jnp.int32),
            DMA((6,)),
            DMA((6, NK)),
            DMA((6, NK)),
            DMA((2, 2, NK)),
            DMA((2, 2, NK)),
            DMA((NK,)),
            DMA((NK,)),
            DMA((NK,)),
            DMA((NK,)),
        ],
        compiler_params=pltpu.CompilerParams(
            collective_id=0, has_side_effects=True, vmem_limit_bytes=20 << 20
        ),
        name="gather_tables",
    )(
        *(
            pltpu.with_memory_space_constraint(value, pltpu.HBM)
            for value in (
                features, self_weight, neigh_weight, block_source, edge_weights, labels.reshape(1, ROWS)
            )
        )
    )


def main_kernel(
    nx, nz, src, sel, t_ref, wide_ref, flip_ref, inv_ref, base_ref, hot_ref, ft_ref, w_ref,
    gs_ref, gn_ref, out_ref,
    mean, resid, spread, run, done, tmsend, g,
    pair, zsend, zgot, ysend, relay, ygot, gpair, total, plane, two, far, part, full,
    ps, pr, zs, zr, ys, yr, rs, rr, gps, gpr, pls, plr, qs, qr, fs, fr, aps, apr, gfs, gfr, word,
):
    me = Place(nx, nz)
    partner = me.partner()
    core, yhi, z = me.core, me.yhi, me.z
    up, down = me.zstep(1), me.zstep(nz - 1)
    yup, ydown = me.ystep(1), me.ystep(3)
    flat = me.x * 4 + me.y
    q, h = z % 2, z // 2
    planes = nx * 4
    beside = me.zto(2 * h + 1 - q)

    def plane_dev(p):
        return me.at(p // 4, p % 4, z, core)

    steps = sorted(
        ((dx, dy) for dx in range(nx) for dy in range(4) if dx or dy),
        key=lambda s: -min(s[0], nx - s[0]) - min(s[1], 4 - s[1]),
    )

    def place(step):
        return (me.x + step[0]) % nx * 4 + (me.y + step[1]) % 4

    near = [me.zstep(d) for d in (1, nz - 1, 2, nz - 2, 3, nz - 3, 4, nz - 4)]
    barrier = signal([plane_dev(place(step)) for step in steps] + near + [partner])

    def others(body):
        @pl.loop(0, planes)
        def _(p):
            @pl.when(p != flat)
            def _():
                body(p)

    started = []

    def go(copy):
        copy.start()
        started.append(copy)

    for b in range(8):
        here = pl.ds(b * BLOCK, BLOCK)
        table = jnp.concatenate([t_ref[src[b, s]] for s in range(8)], axis=0)
        m = dot(wide_ref[here, :], table) * inv_ref[here, :]
        mean[0, here, :], mean[1, here, :] = split(m)
    wn, ws = (w_ref[0], w_ref[1]), (w_ref[2], w_ref[3])
    logits = base_ref[...] + dot3((mean[0], mean[1]), wn)
    resid[0], resid[1] = split(1.0 / (1.0 + jnp.exp(-logits)) - hot_ref[...])

    halves = (1 - yhi, yhi)

    def pair_grad(i):
        here = pl.ds(i * 256, 256)
        return remote(g.at[1 - core, here], gpair.at[here], gps.at[i], gpr.at[i], partner)

    def weight_grad(i):
        if i == 0:
            value = dot3((ft_ref[0], ft_ref[1]), (resid[0], resid[1]))
        else:
            value = dot3((mean[0], mean[1]), (resid[0], resid[1]), TURN)
        for c in (0, 1):
            g[c, i * 256 : (i + 1) * 256, :] = value[:, c * 128 : (c + 1) * 128]

    weight_grad(0)
    pl.semaphore_wait(barrier, planes + len(near))
    pair_grad(0).start()
    for dev in near[6:]:
        pl.semaphore_signal(word, inc=1, device_id=dev, device_id_type=MESH)
    weight_grad(1)
    pair_grad(1).start()

    def block_terms(reg, r, k):
        found = []
        for j in range(CH // BLOCK):
            t = reg * 32 + r * 8 + k * (CH // BLOCK) + j
            found.append(done[sel[2, t]].astype(F32) * sel[3, t].astype(F32))
        return jnp.concatenate(found, axis=0)

    def pair_out(reg, half, k):
        at = reg * 2 + half
        tmsend[at, rows(k), :] = block_terms(reg, halves[half] * 2 + 1 - core, k).astype(BF)
        go(
            remote(
                tmsend.at[at, rows(k)], pair.at[at, rows(k)], ps.at[at, k], pr.at[at, k], partner
            )
        )

    def pair_sum(reg, half, k):
        ref = pair.at[reg * 2 + half, rows(k)]
        mine = block_terms(reg, halves[half] * 2 + core, k)
        remote(ref, ref, ps.at[reg * 2 + half, k], pr.at[reg * 2 + half, k], partner).wait_recv()
        return mine + pair[reg * 2 + half, rows(k), :].astype(F32)

    def z_out(half, k):
        for d in (0, 1):
            zsend[d * 2 + half, rows(k), :] = pair_sum(1 + d, half, k).astype(BF)
            go(
                remote(
                    zsend.at[d * 2 + half, rows(k)],
                    zgot.at[d * 2 + half, rows(k)],
                    zs.at[d * 2 + half, k],
                    zr.at[d * 2 + half, k],
                    (down, up)[d],
                )
            )

    def region_sum(half, k):
        value = pair_sum(0, half, k)
        for d in (0, 1):
            ref = zgot.at[d * 2 + half, rows(k)]
            remote(ref, ref, zs.at[d * 2 + half, k], zr.at[d * 2 + half, k], up).wait_recv()
            value = value + zgot[d * 2 + half, rows(k), :].astype(F32)
        return value

    def ydev(k):
        return yup if k < 2 else ydown

    def y_out(k):
        ysend[rows(k), :] = region_sum(0, k).astype(BF)
        go(remote(ysend.at[rows(k)], relay.at[rows(k)], ys.at[k], rr.at[k], ydev(k)))

    def relay_on(k):
        ref = relay.at[rows(k)]
        remote(ref, ref, ys.at[k], rr.at[k], yup).wait_recv()
        go(remote(ref, ygot.at[rows(k)], rs.at[k], yr.at[k], ydev(k)))

    def finish(k):
        value = region_sum(1, k) + out_ref[rows(k), :]
        ref = ygot.at[rows(k)]
        remote(ref, ref, rs.at[k], yr.at[k], yup).wait_recv()
        out_ref[rows(k), :] = value + ygot[rows(k), :].astype(F32)

    width = ROWS // planes

    def piece(p):
        return pl.ds(pl.multiple_of(p * width, width), width)

    def plane_copy(i):
        p = place(steps[i])
        return remote(total.at[piece(p)], plane.at[flat], pls.at[i], plr.at[flat], plane_dev(p))

    def plane_out(i):
        here = pl.ds(i * 256, 256)
        pair_grad(i).wait_recv()
        total[here, :] = (g[core, here, :] + gpair[here, :]).astype(BF)
        for j in range(planes - 1):

            @pl.when(place(steps[j]) * 2 // planes == i)
            def _():
                plane_copy(j).start()

    plane_out(0)
    value = dot3((resid[0], resid[1]), wn, LAST) * inv_ref[...]
    spread[...] = value.astype(BF).reshape(8, BLOCK, 256)
    plane_out(1)

    run[...] = jnp.zeros((BLOCK, 256), F32)

    @pl.loop(0, 64, unroll=4)
    def _(r):
        at = sel[0, r]
        value = dot(flip_ref[at], spread[at // 8]) + run[...] * sel[1, r].astype(F32)
        run[...] = value
        done[r] = value.astype(BF)

    for k in ORDER:
        pair_out(1, 0, k)
        pair_out(2, 0, k)
    for k in ORDER:
        pair_out(0, 0, k)
    for k in ORDER:
        pair_out(1, 1, k)
        pair_out(2, 1, k)
    for k in ORDER:
        pair_out(0, 1, k)

    plane[flat] = total[piece(flat), :]

    @others
    def _(p):
        remote(plane.at[p], plane.at[p], pls.at[p], plr.at[p], partner).wait_recv()

    summed = plane[0].astype(F32)
    for p in range(1, planes):
        summed = summed + plane[p].astype(F32)
    part[...] = summed.reshape(2, width // 2, 128)
    two_copy = remote(part.at[1 - q], two, qs.at[0], qr.at[0], beside)
    two_copy.start()
    out_ref[...] = dot3((resid[0], resid[1]), ws, LAST)
    two_copy.wait_recv()
    far[z] = (part[q] + two[...]).astype(BF)

    def far_copy(d):
        return remote(far.at[z], far.at[z], fs.at[d], fr.at[d], me.zstep(d))

    pl.semaphore_wait(word, 2)
    for d in sorted(range(1, nz), key=lambda d: -min(d, nz - d)):
        far_copy(d).start()
    for k in ORDER:
        z_out(0, k)
    y_out(0)
    y_out(2)
    for d in range(1, nz):
        ref = far.at[(z + nz - d) % nz]
        remote(ref, ref, fs.at[d], fr.at[d], partner).wait_recv()
    tile = width // 2
    for j in (0, 1):
        summed = far[j].astype(F32)
        for i in range(j + 2, nz, 2):
            summed = summed + far[i].astype(F32)
        here = pl.ds(pl.multiple_of(flat * width + j * tile, tile), tile)
        full[core, here, :] = summed.astype(BF)
    mine = full.at[core, piece(flat)]

    def spread_copy(i):
        return remote(mine, mine, aps.at[i], apr.at[flat], plane_dev(place(steps[i])))

    def last_copy(p):
        ref = full.at[core, piece(p)]
        return remote(ref, ref, gfs.at[p], gfr.at[p], partner)

    for i in range(planes - 1):
        spread_copy(i).start()
    last_copy(flat).start()
    for k in ORDER:
        z_out(1, k)
    y_out(1)
    y_out(3)
    for k in ORDER:
        relay_on(k)

    @others
    def _(p):
        ref = full.at[core, piece(p)]
        remote(ref, ref, aps.at[p], apr.at[p], partner).wait_recv()
        last_copy(p).start()

    for k in ORDER:
        finish(k)

    @pl.loop(0, planes)
    def _(p):
        ref = full.at[1 - core, piece(p)]
        remote(ref, ref, gfs.at[p], gfr.at[p], partner).wait_recv()

    for i, ref in enumerate((gs_ref, gn_ref)):
        for c in (0, 1):
            ref[:, c * 128 : (c + 1) * 128] = full[c, i * 256 : (i + 1) * 256, :].astype(F32)

    for i in (0, 1):
        pair_grad(i).wait_send()
    two_copy.wait_send()
    for d in range(1, nz):
        far_copy(d).wait_send()

    for i in range(planes - 1):
        plane_copy(i).wait_send()
        spread_copy(i).wait_send()

    @pl.loop(0, planes)
    def _(p):
        last_copy(p).wait_send()

    for copy in started:
        copy.wait_send()


def main(nx, nz, block_source, table, wide, flip, inv, base, hot, turned, weights, sel):
    planes = nx * 4
    width = ROWS // planes
    big = (6, NK)
    return pl.pallas_call(
        functools.partial(main_kernel, nx, nz),
        out_shape=(
            jax.ShapeDtypeStruct((256, 256), F32),
            jax.ShapeDtypeStruct((256, 256), F32),
            jax.ShapeDtypeStruct((ROWS, 256), F32),
        ),
        in_specs=[SM, SM] + [VM] * 8,
        out_specs=(VM,) * 3,
        scratch_shapes=[
            pltpu.VMEM((2, ROWS, 256), BF),
            pltpu.VMEM((2, ROWS, 256), BF),
            pltpu.VMEM((8, BLOCK, 256), BF),
            pltpu.VMEM((BLOCK, 256), F32),
            pltpu.VMEM((64, BLOCK, 256), BF),
            pltpu.VMEM((6, ROWS, 256), BF),
            pltpu.VMEM((2, ROWS, 128), F32),
            pltpu.VMEM((6, ROWS, 256), BF),
            pltpu.VMEM((4, ROWS, 256), BF),
            pltpu.VMEM((4, ROWS, 256), BF),
            pltpu.VMEM((ROWS, 256), BF),
            pltpu.VMEM((ROWS, 256), BF),
            pltpu.VMEM((ROWS, 256), BF),
            pltpu.VMEM((ROWS, 128), F32),
            pltpu.VMEM((ROWS, 128), BF),
            pltpu.VMEM((planes, width, 128), BF),
            pltpu.VMEM((width // 2, 128), F32),
            pltpu.VMEM((nz, width // 2, 128), BF),
            pltpu.VMEM((2, width // 2, 128), F32),
            pltpu.VMEM((2, ROWS, 128), BF),
            DMA(big), DMA(big), DMA((4, NK)), DMA((4, NK)),
            DMA((NK,)), DMA((NK,)), DMA((NK,)), DMA((NK,)),
            DMA((2,)), DMA((2,)), DMA((planes,)), DMA((planes,)),
            DMA((1,)), DMA((1,)), DMA((nz,)), DMA((nz,)),
            DMA((planes,)), DMA((planes,)),
            DMA((planes,)), DMA((planes,)),
            pltpu.SemaphoreType.REGULAR,
        ],
        compiler_params=pltpu.CompilerParams(
            collective_id=1, has_side_effects=True, vmem_limit_bytes=30 << 20
        ),
        name="main_math",
    )(block_source, sel, table.reshape(96, BLOCK, 256), wide, flip, inv, base, hot, turned, weights)


def store_kernel(a, b, c, a_hbm, b_hbm, c_hbm, sems):
    copies = [
        pltpu.make_async_copy(src, dst, sems.at[i])
        for i, (src, dst) in enumerate(((c, c_hbm), (a, a_hbm), (b, b_hbm)))
    ]
    for copy in copies:
        copy.start()
    for copy in copies:
        copy.wait()


def store(*values):
    return pl.pallas_call(
        store_kernel,
        out_shape=tuple(jax.ShapeDtypeStruct(v.shape, v.dtype) for v in values),
        in_specs=[VM] * 3,
        out_specs=(pl.BlockSpec(memory_space=pltpu.HBM),) * 3,
        scratch_shapes=[DMA((3,))],
        compiler_params=pltpu.CompilerParams(vmem_limit_bytes=8 << 20),
        name="store_results",
    )(*values)


def solution(mesh):
    nx, nz = mesh.shape["row"] // 2, mesh.shape["col"]
    split_rows = P(("row", "col", "rep"))

    def on_device(features, self_weight, neigh_weight, block_source, edge_weights, labels):
        prepared = gather(
            nx, nz, features, self_weight, neigh_weight, block_source, edge_weights, labels
        )
        return store(*main(nx, nz, block_source, *prepared))

    return jax.shard_map(
        on_device,
        mesh=mesh,
        in_specs=(split_rows, P(), P(), split_rows, split_rows, split_rows),
        out_specs=(P(), P(), split_rows),
        check_vma=False,
    )
```
